32 devices in a mesh: grp: 4 (over y, x), tile: 8 (over z, core).
Axes of the slice: x: 2, y: 2, z: 4, core: 2. Of those that a mesh axis runs over, the one named last changes fastest.
Arguments:
- flow_fields: float32 [5, 256, 16, 128], P(None, 'tile', 'grp'), may hold values from -6 to 6
- turbulent_diffusivity: float32 [256, 16, 128], P('tile', 'grp'), may hold values from 0.05 to 0.3
- holder_unit: int32 [4, 256, 1], P('grp', 'tile'), may hold values from 0 to 7, as said below
- spray_volume_position: int32 [8, 1024, 128], P('tile'), may hold values from 0 to 511
- patch_pick_unreduced: int32 [8, 1024], P('tile'), may hold values from 0 to 1048575
- droplet_motion: float32 [8, 1024, 3, 128], P('tile'), may hold values from -6 to 6
- droplet_warmth: float32 [8, 1024, 128], P('tile'), may hold values from -6 to 6
- droplet_weightiness: float32 [8, 1024, 128], P('tile'), may hold values from 0.25 to 2
- droplet_multiplicity: float32 [8, 1024, 128], P('tile'), may hold values from 0.5 to 2
- living_spray_batches: int32 [8], P('tile'), may hold values from 1 to 1024, 4096 in all
Outputs:
- gas_next: float32 [5, 256, 16, 128], P(None, 'tile', 'grp')
The draws below stay inside these ranges and needn't reach their ends.
Inputs may be any that keep to these rules, and one draw needn't show every extreme that they name: `holder_unit`: among the 32 tiles of one gas device (aligned blocks of 32 rows of owner, in order of its first two dimensions) no parcel device owns more than 8, and in every such block one parcel device owns exactly 8. Two parcel devices own no tile at all. Rows with g = 3 are not used. `living_spray_batches`: live blocks of a device are its first ones; the busiest parcel device has exactly 1024, and they sum to 4096.
All inputs are finite; a program needn't handle non-finite values.
Results may differ from the reference program's by a relative error of at most 0.0045.
Values may be sent and summed in bfloat16 or wider, within the bound.
A program may use at most 64 MiB of HBM per device.

```python
import math
import jax
import jax.numpy as jnp
import numpy as np

NF = 5
GROUP_DROPLETS = 128
BY = 4
BZ = 128
BX = 32
UNIT_BATCHES = 1024
SPRAY_UNITS = 8
NX = 256
NY = 16
GAS_Y = 12
SLOTS = 8
N_GRP = 4


def draw_holder_unit(key, part):
    block_count = NY // BY * (NX // BX)
    spare_count = SPRAY_UNITS - 2
    key_order, key_blocks, key_rows = jax.random.split(jax.random.fold_in(key, 7), 3)
    middle = (1 + jax.random.permutation(key_order, SPRAY_UNITS - 2)).astype(jnp.int32)
    allowed = jnp.concatenate([jnp.array([0, SPRAY_UNITS - 1], dtype=jnp.int32), middle[2:]])
    shuffles = jax.vmap(lambda subkey: jax.random.permutation(subkey, spare_count))(jax.random.split(key_blocks, block_count)).astype(jnp.int32)
    first_block = jnp.arange(block_count, dtype=jnp.int32)[:, None] == 0
    shuffles = jnp.where(first_block, jnp.arange(spare_count, dtype=jnp.int32)[None, :], shuffles)
    places = jnp.arange(BX, dtype=jnp.int32)
    column = jnp.where(places < SLOTS, 0, 1 + (places - SLOTS) % (spare_count - 1)).astype(jnp.int32)
    labels = allowed[jnp.take(shuffles, column, axis=1)]
    row_order = jax.vmap(lambda subkey: jax.random.permutation(subkey, BX))(jax.random.split(key_rows, block_count)).astype(jnp.int32)
    labels = jnp.take_along_axis(labels, row_order, axis=1)
    return labels.reshape(NY // BY, NX, 1).astype(jnp.int32)


def with_ends(entries, rng, low, high):
    index_at = [jax.random.randint(jax.random.fold_in(rng, axis), (), 0, length) for axis, length in enumerate(entries.shape)]
    widest = entries.shape.index(max(entries.shape))
    next_to = index_at[:widest] + [(index_at[widest] + 1) % entries.shape[widest]] + index_at[widest + 1:]
    return entries.at[tuple(index_at)].set(low).at[tuple(next_to)].set(high)


def shard_levels(rng, dims, cuts, least, high):
    loudness = 1.0
    for dim, shards_of in cuts:
        draws = jax.random.uniform(jax.random.fold_in(jax.random.fold_in(rng, 6), dim), (shards_of,), jnp.float32, least / len(cuts), high / len(cuts))
        loudness = loudness * jnp.repeat(jnp.exp(draws), dims[dim] // shards_of).reshape((-1,) + (1,) * (len(dims) - 1 - dim))
    return loudness


def split_up(amount, total, limit, skew):
    weights = [(1 << 20) // math.isqrt(rank ** skew) + 1 for rank in range(2, amount + 1)]
    rest, given = total - limit - (amount - 1), [1] * (amount - 1)
    while rest > 0:
        free = [i for i in range(amount - 1) if given[i] < limit]
        mass, budget = sum([weights[i] for i in free]), rest
        for i in free:
            extra = min(limit - given[i], max(1, budget * weights[i] // mass), rest)
            given[i] = given[i] + extra
            rest = rest - extra
    return np.array([limit] + given)


def uneven(stream_key, count, total, reach, skew):
    if count == 2:
        one = jax.random.randint(stream_key, (), max(1, total - reach), min(reach, total - 1) + 1)
        return jnp.stack([one, total - one])
    tallies = jnp.asarray(split_up(count, total, reach, skew), jnp.int32)
    twos = (count - 1) // 2
    source_of, receiver = tallies[1:1 + 2 * twos:2], tallies[2:2 + 2 * twos:2]
    margin = jnp.minimum(source_of - 1, reach - receiver)
    passed = jax.random.randint(jax.random.fold_in(stream_key, 1), (twos,), 0, 1 << 20) % (margin + 1)
    tallies = tallies.at[1:1 + 2 * twos:2].set(source_of - passed).at[2:2 + 2 * twos:2].set(receiver + passed)
    return tallies[jax.random.permutation(jax.random.fold_in(stream_key, 2), count)]


def scatter_about(key, shape, scale, bound, pieces=(), kind=jnp.bfloat16):
    level = shard_levels(key, shape, pieces, -0.22, 0.18) if pieces else 1.0
    drawn = jax.random.normal(key, shape, jnp.float32) * scale * level
    return jnp.minimum(jnp.maximum(drawn, -bound), bound).astype(kind)


def setup_inputs(seed: int = 0) -> dict:
    keys = jax.random.split(jax.random.key(seed), 11)
    flow_fields = scatter_about(keys[0], (NF, NX, NY, BZ), 1.0, 6.0, ((1, 8), (2, 4)), jnp.float32)
    turbulent_diffusivity = jnp.clip(jnp.exp(math.log(0.3) - 1.7917595 * jax.random.uniform(keys[1], (NX, NY, BZ), jnp.float32) ** shard_levels(keys[1], (NX, NY, BZ), ((0, 8), (1, 4)), -0.2, 0.2)), 0.05, 0.3)
    holder_unit = draw_holder_unit(jax.random.fold_in(keys[10], 71), 0)
    spray_volume_position = with_ends(jax.random.randint(keys[3], (SPRAY_UNITS, UNIT_BATCHES, GROUP_DROPLETS), 0, BY * BZ), jax.random.fold_in(keys[3], 1), 0, (BY * BZ) - 1).astype(jnp.int32)
    patch_pick_unreduced = with_ends(jax.random.randint(keys[4], (SPRAY_UNITS, UNIT_BATCHES), 0, 1048576), jax.random.fold_in(keys[4], 1), 0, 1048575).astype(jnp.int32)
    droplet_motion = scatter_about(keys[5], (SPRAY_UNITS, UNIT_BATCHES, 3, GROUP_DROPLETS), 1.0, 6.0, ((0, 8),), jnp.float32)
    droplet_warmth = scatter_about(keys[6], (SPRAY_UNITS, UNIT_BATCHES, GROUP_DROPLETS), 1.0, 6.0, ((0, 8),), jnp.float32)
    droplet_weightiness = jnp.clip(jnp.exp(math.log(2.0) - 2.0794415 * jax.random.uniform(keys[7], (SPRAY_UNITS, UNIT_BATCHES, GROUP_DROPLETS), jnp.float32) ** shard_levels(keys[7], (SPRAY_UNITS, UNIT_BATCHES, GROUP_DROPLETS), ((0, 8),), -0.2, 0.2)), 0.25, 2.0)
    droplet_multiplicity = jnp.clip(jnp.exp(math.log(2.0) - 1.3862944 * jax.random.uniform(keys[8], (SPRAY_UNITS, UNIT_BATCHES, GROUP_DROPLETS), jnp.float32) ** shard_levels(keys[8], (SPRAY_UNITS, UNIT_BATCHES, GROUP_DROPLETS), ((0, 8),), -0.2, 0.2)), 0.5, 2.0)
    living_spray_batches = uneven(keys[9], SPRAY_UNITS, SPRAY_UNITS * UNIT_BATCHES // 2, UNIT_BATCHES, 2).astype(jnp.int32)
    return dict(flow_fields=flow_fields, turbulent_diffusivity=turbulent_diffusivity, holder_unit=holder_unit, spray_volume_position=spray_volume_position, patch_pick_unreduced=patch_pick_unreduced, droplet_motion=droplet_motion, droplet_warmth=droplet_warmth, droplet_weightiness=droplet_weightiness, droplet_multiplicity=droplet_multiplicity, living_spray_batches=living_spray_batches)


def droplet_coupling_feeds(reached_markers, droplet_motion, droplet_warmth, droplet_weightiness, droplet_multiplicity):
    gas_velocity = reached_markers[..., 0:3, :]
    fluid_warming_share = reached_markers[..., 3, :]
    gas_fuel = reached_markers[..., 4, :]
    relative = gas_velocity - droplet_motion
    speed_sq = jnp.sum(relative * relative, axis=-2)
    surface = droplet_weightiness ** (2.0 / 3.0)
    inverse_tau = 0.8 * (1.0 + 0.15 * (1.0 + speed_sq) ** 0.3435) / surface
    relaxation = 1.0 - jnp.exp(-0.5 * inverse_tau)
    new_velocity = droplet_motion + relaxation[..., None, :] * relative
    heating = 1.0 / (1.0 + jnp.exp(-(fluid_warming_share - gas_fuel)))
    leftover_liquid_load = jnp.exp(-0.3 * heating / surface)
    updated_droplet_load = droplet_weightiness * leftover_liquid_load
    warming_speed = 1.0 - jnp.exp(-0.25 * inverse_tau)
    updated_droplet_warmth = droplet_warmth + warming_speed * (fluid_warming_share - droplet_warmth) - 0.5 * (1.0 - leftover_liquid_load)
    momentum = droplet_weightiness[..., None, :] * droplet_motion - updated_droplet_load[..., None, :] * new_velocity
    enthalpy_content = droplet_weightiness * droplet_warmth - updated_droplet_load * updated_droplet_warmth
    stacked = jnp.concatenate([momentum, enthalpy_content[..., None, :], (droplet_weightiness - updated_droplet_load)[..., None, :]], axis=-2)
    return droplet_multiplicity[..., None, :] * stacked


def reference(flow_fields, turbulent_diffusivity, holder_unit, spray_volume_position, patch_pick_unreduced, droplet_motion, droplet_warmth, droplet_weightiness, droplet_multiplicity, living_spray_batches):
    gas_rows = GAS_Y
    groups = N_GRP - 1
    tile_cells = BY * BZ
    gas_field = flow_fields[:, :, :gas_rows, :]
    nu_field = turbulent_diffusivity[:, :gas_rows, :]
    padded = jnp.pad(gas_field, ((0, 0), (1, 1), (1, 1), (1, 1)))
    beside = padded[:, 2:, 1:-1, 1:-1] + padded[:, :-2, 1:-1, 1:-1]
    beside = beside + padded[:, 1:-1, 2:, 1:-1] + padded[:, 1:-1, :-2, 1:-1]
    beside = beside + padded[:, 1:-1, 1:-1, 2:] + padded[:, 1:-1, 1:-1, :-2]
    laplace = beside - 6.0 * gas_field
    tiles = gas_field.astype(jnp.bfloat16).reshape(NF, NX, groups, BY, BZ)
    tiles = tiles.transpose(2, 1, 0, 3, 4).reshape(groups * NX, NF, tile_cells)
    plane_owner = holder_unit[:groups, :, 0].reshape(groups * NX)
    owned = plane_owner[None, :] == jnp.arange(SPRAY_UNITS, dtype=jnp.int32)[:, None]
    owned_count = jnp.sum(owned.astype(jnp.int32), axis=1)
    listing = jnp.argsort(jnp.where(owned, 0, 1).astype(jnp.int32), axis=1, stable=True).astype(jnp.int32)
    picked = (patch_pick_unreduced % jnp.maximum(owned_count, 1)[:, None]).astype(jnp.int32)
    block_tile = jnp.take_along_axis(listing, picked, axis=1)
    alive = (jnp.arange(UNIT_BATCHES, dtype=jnp.int32)[None, :] < living_spray_batches[:, None]) & (owned_count[:, None] > 0)
    reached_markers = tiles[block_tile[:, :, None], :, spray_volume_position].astype(jnp.float32).transpose(0, 1, 3, 2)
    coupling_feeds = droplet_coupling_feeds(reached_markers, droplet_motion, droplet_warmth, droplet_weightiness, droplet_multiplicity)
    coupling_feeds = coupling_feeds * alive[:, :, None, None].astype(jnp.float32)
    deposit = jnp.zeros((groups * NX, NF, tile_cells), jnp.float32)
    deposit = deposit.at[block_tile[:, :, None], :, spray_volume_position].add(coupling_feeds.transpose(0, 1, 3, 2))
    placed = deposit.reshape(groups, NX, NF, BY, BZ).transpose(2, 1, 0, 3, 4).reshape(NF, NX, gas_rows, BZ)
    advanced = gas_field + 0.5 * nu_field * laplace + placed
    return jnp.concatenate([advanced, jnp.zeros((NF, NX, BY, BZ), jnp.float32)], axis=2)
```

```python
import functools

import jax
import jax.numpy as jnp
from jax import lax
from jax.experimental import pallas as pl
from jax.experimental.pallas import tpu as pltpu
from jax.sharding import PartitionSpec as P

MESH = pl.DeviceIdType.MESH
SLOTS = 8
BATCH = 16
VMEM = pl.BlockSpec(memory_space=pltpu.VMEM)
SMEM = pl.BlockSpec(memory_space=pltpu.SMEM)
F32, BF16, I32 = jnp.float32, jnp.bfloat16, jnp.int32


def pack_kernel(owners, col_ref, row_ref, gas_ref, send_ref, sel_ref):
    planes = row_ref.shape[1]
    col, row = col_ref[...], row_ref[...]
    s = lax.broadcasted_iota(I32, (planes, planes), 0)
    l = lax.broadcasted_iota(I32, (planes, planes), 1)
    earlier = jnp.where((col == row) & (s < l), 1, 0)
    rank = jnp.sum(earlier, axis=0, keepdims=True)
    target = lax.broadcasted_iota(I32, (owners * SLOTS, planes), 0)
    sel = jnp.where(row * SLOTS + rank == target, 1.0, 0.0).astype(BF16)
    sel_ref[...] = sel
    rows = gas_ref.shape[0]
    for r in range(0, rows, 2):
        a = jnp.dot(sel, gas_ref[r], preferred_element_type=F32)
        b = jnp.dot(sel, gas_ref[r + 1], preferred_element_type=F32)
        for o in range(owners):
            lo, hi = o * SLOTS, (o + 1) * SLOTS
            both = jnp.concatenate([a[lo:hi], b[lo:hi]], axis=0).astype(BF16)
            send_ref[o, r * SLOTS : (r + 2) * SLOTS, :] = both


def greet(peers):
    barrier = pltpu.get_barrier_semaphore()
    for peer in peers:
        pl.semaphore_signal(barrier, inc=1, device_id=peer, device_id_type=MESH)
    pl.semaphore_wait(barrier, len(peers))


def exchange_kernel(
    ng, nt, nf, send_ref, gas_ref, first_ref, last_ref, own_ref,
    recv_ref, ylo_ref, yhi_ref, xlo_ref, xhi_ref, all_ref,
    tile_s, tile_r, own_s, own_r, own2_s, own2_r, halo_s, halo_r, local_sem,
):
    g, t = lax.axis_index("grp"), lax.axis_index("tile")
    grp_peers = [(lax.rem(g + k, ng), t) for k in range(1, ng)]
    tile_peers = [(g, lax.rem(t + k, nt)) for k in range(1, nt)]
    greet(grp_peers + tile_peers)

    def copy(src, dst, ss, rs, dev):
        c = pltpu.make_async_remote_copy(
            src_ref=src, dst_ref=dst, send_sem=ss, recv_sem=rs, device_id=dev, device_id_type=MESH
        )
        c.start()
        return c

    own_copies = [
        copy(own_ref.at[0], all_ref.at[t, g], own_s.at[k], own_r.at[k], peer)
        for k, peer in enumerate(grp_peers)
    ]
    mine = pltpu.make_async_copy(own_ref.at[0], all_ref.at[t, g], local_sem.at[0])
    mine.start()
    slab = pltpu.make_async_copy(send_ref.at[t], recv_ref.at[t], local_sem.at[1])
    slab.start()
    rows = gas_ref.shape[0]
    others = [
        copy(gas_ref.at[pl.ds(rows - nf, nf)], ylo_ref, halo_s.at[0], halo_r.at[0], grp_peers[0]),
        copy(gas_ref.at[pl.ds(0, nf)], yhi_ref, halo_s.at[1], halo_r.at[1], grp_peers[-1]),
        copy(last_ref, xlo_ref, halo_s.at[2], halo_r.at[2], tile_peers[0]),
        copy(first_ref, xhi_ref, halo_s.at[3], halo_r.at[3], tile_peers[-1]),
    ]
    for k, peer in enumerate(tile_peers):
        others.append(copy(send_ref.at[peer[1]], recv_ref.at[t], tile_s.at[k], tile_r.at[k], peer))
    mine.wait()
    for c in own_copies:
        c.wait()
    for k, peer in enumerate(tile_peers):
        others.append(copy(all_ref.at[t], all_ref.at[t], own2_s.at[k], own2_r.at[k], peer))
    slab.wait()
    for c in others:
        c.wait()


def parcel_kernel(
    ng, nt, nf, scal_ref, recv_ref, own_ref, pick_ref, pos_ref, mot_ref, warm_ref, mass_ref, mult_ref,
    dep_ref,
    stage, table, acc, seen, par, src, hot, ints, smem, slot_of, todo, sem,
):
    g, p, live = scal_ref[0], scal_ref[1], scal_ref[2]
    slots = nt * SLOTS
    blocks = pos_ref.shape[0]
    shift = blocks.bit_length() - 1
    prow = blocks // 128
    owned = jnp.where(own_ref[...] == p, 1, 0)
    counts = jnp.sum(owned, axis=1, keepdims=True)
    which = lax.broadcasted_iota(I32, counts.shape, 0)
    counts = jnp.where(lax.rem(which, ng) < ng - 1, counts, 0)
    total = jnp.maximum(jnp.sum(counts, axis=0, keepdims=True), 1)
    pick = pick_ref[...]
    total_f = total.astype(F32)
    quotient = jnp.floor(pick.astype(F32) / total_f).astype(I32)
    left = pick - quotient * total
    left = jnp.where(left < 0, left + total, left)
    left = jnp.where(left >= total, left - total, left)
    ints[0:prow, :] = left
    ints[prow : prow + ng * nt, :] = jnp.broadcast_to(counts, (ng * nt, 128))
    to_smem = pltpu.make_async_copy(ints, smem, sem)
    to_smem.start()
    rows = recv_ref.shape[1] // SLOTS
    stage[...] = jnp.zeros_like(stage)
    for d in range(nt):
        for r in range(0, rows, 2):
            both = recv_ref[d, r * SLOTS : (r + 2) * SLOTS, :].astype(F32)
            for h in range(2):
                row = (r + h) // nf * 8 + (r + h) % nf
                stage[pl.ds(d * SLOTS * 32 + row, SLOTS, stride=32), :] = both[h * SLOTS : (h + 1) * SLOTS]

    @pl.loop(0, slots + 1)
    def _(i):
        table[i] = stage[pl.ds(pl.multiple_of(i * 32, 32), 32), :].astype(BF16)

    acc[...] = jnp.zeros_like(acc)
    src[...] = jnp.zeros_like(src)
    to_smem.wait()

    def per_device(i, carry):
        total_seen, low, high = carry
        gg, d = i // nt, lax.rem(i, nt)
        count = smem[prow + d * ng + gg, 0]
        here = gg == g

        @pl.when(here)
        def _():
            for j in range(SLOTS):
                slot_of[total_seen - low + j] = d * SLOTS + j

        after = total_seen + count
        low = jnp.where(gg < g, after, low)
        high = jnp.where(gg <= g, after, high)
        return after, low, high

    zero = jnp.int32(0)
    _, low, high = lax.fori_loop(0, (ng - 1) * nt, per_device, (zero, zero, zero))
    slot_of[slots + SLOTS] = slots

    def compact(i, n):
        for j in range(8):
            b = i * 8 + j
            k = smem[b // 128, lax.rem(b, 128)]
            todo[n] = ((k - low) << shift) + b
            n = n + jnp.where((k >= low) & (k < high) & (b < live), 1, 0)
        return n

    n = lax.fori_loop(0, (live + 7) // 8, compact, zero)
    for j in range(BATCH):
        todo[n + j] = (slots + SLOTS) << shift

    sub = lax.broadcasted_iota(I32, (128, 128), 0)

    @pl.loop(0, (n + BATCH - 1) // BATCH)
    def _(step):
        where_at, ys = [], []
        for j in range(BATCH):
            v = todo[step * BATCH + j]
            b = v & (blocks - 1)
            slot = slot_of[v >> shift]
            cell = pos_ref[pl.ds(b, 1), :]
            y = cell >> 7
            one = jnp.where(sub == (cell & 127), 1.0, 0.0).astype(BF16)
            hot[j] = one
            got = jnp.dot(table[slot], one, preferred_element_type=F32)
            upper = jnp.where(y < 1, got[0:8], got[8:16])
            lower = jnp.where(y < 3, got[16:24], got[24:32])
            seen[pl.ds(j * 8, 8), :] = jnp.where(y < 2, upper, lower)
            par[0:3, j, :] = mot_ref[b]
            par[3:4, j, :] = warm_ref[pl.ds(b, 1), :]
            par[4:5, j, :] = mass_ref[pl.ds(b, 1), :]
            par[5:6, j, :] = mult_ref[pl.ds(b, 1), :]
            where_at.append(slot)
            ys.append(y)
        field = [seen[pl.ds(f, BATCH, stride=8), :] for f in range(5)]
        v0, v1, v2, warm, mass, mult = [par[f] for f in range(6)]
        r0, r1, r2 = field[0] - v0, field[1] - v1, field[2] - v2
        speed_sq = r0 * r0 + r1 * r1 + r2 * r2
        inv_surface = jnp.exp(jnp.log(mass) * (-2.0 / 3.0))
        inverse_tau = 0.8 * (1.0 + 0.15 * jnp.exp(0.3435 * jnp.log(1.0 + speed_sq))) * inv_surface
        relax = 1.0 - jnp.exp(-0.5 * inverse_tau)
        heating = 1.0 / (1.0 + jnp.exp(field[4] - field[3]))
        remain = jnp.exp(-0.3 * heating * inv_surface)
        new_mass = mass * remain
        warming = 1.0 - jnp.exp(-0.25 * inverse_tau)
        new_warm = warm + warming * (field[3] - warm) - 0.5 * (1.0 - remain)
        outs = [mass * v - new_mass * (v + relax * r) for v, r in ((v0, r0), (v1, r1), (v2, r2))]
        outs += [mass * warm - new_mass * new_warm, mass - new_mass]
        for f, o in enumerate(outs):
            src[pl.ds(f, BATCH, stride=8), :] = mult * o
        added = []
        for j in range(BATCH):
            s8 = src[pl.ds(j * 8, 8), :]
            s32 = jnp.concatenate([jnp.where(ys[j] == k, s8, 0.0) for k in range(4)], axis=0).astype(BF16)
            added.append(
                lax.dot_general(s32, hot[j], (((1,), (1,)), ((), ())), preferred_element_type=F32)
            )
        for j in range(BATCH):
            at = pl.ds(pl.multiple_of(where_at[j] * 32, 32), 32)
            acc[at, :] = acc[at, :] + added[j]

    for d in range(nt):
        for r in range(0, rows, 2):
            pair = [
                acc[pl.ds(d * SLOTS * 32 + q // nf * 8 + q % nf, SLOTS, stride=32), :] for q in (r, r + 1)
            ]
            dep_ref[d, r * SLOTS : (r + 2) * SLOTS, :] = jnp.concatenate(pair, axis=0).astype(BF16)


def finish_kernel(
    ng, nt, nf, dep_ref, selt_ref, gas_ref, nu_ref, ylo_ref, yhi_ref, xlo_ref, xhi_ref,
    out_ref, recv, tile_s, tile_r, local_sem,
):
    g, t = lax.axis_index("grp"), lax.axis_index("tile")
    peers = [(g, lax.rem(t + k, nt)) for k in range(1, nt)]
    greet(peers)
    copies = []
    for k, peer in enumerate(peers):
        c = pltpu.make_async_remote_copy(
            src_ref=dep_ref.at[peer[1]], dst_ref=recv.at[t], send_sem=tile_s.at[k],
            recv_sem=tile_r.at[k], device_id=peer, device_id_type=MESH,
        )
        c.start()
        copies.append(c)
    slab = pltpu.make_async_copy(dep_ref.at[t], recv.at[t], local_sem)
    slab.start()
    rows, planes, width = gas_ref.shape
    sub = lax.broadcasted_iota(I32, (planes, width), 0)
    lane = lax.broadcasted_iota(I32, (planes, width), 1)
    gas_side = jnp.where(g < ng - 1, 1.0, 0.0).astype(F32)
    has_low = jnp.where(t > 0, 1.0, 0.0).astype(F32)
    has_high = jnp.where(t < nt - 1, 1.0, 0.0).astype(F32)
    x_low = xlo_ref[...].astype(F32) * has_low
    x_high = xhi_ref[...].astype(F32) * has_high
    for r in range(rows):
        mid = gas_ref[r]
        below = gas_ref[r - nf] if r >= nf else ylo_ref[r].astype(F32)
        above = gas_ref[r + nf] if r < rows - nf else yhi_ref[r - (rows - nf)].astype(F32)
        total = below + above
        total += jnp.where(sub == 0, x_low[r : r + 1], pltpu.roll(mid, 1, 0))
        total += jnp.where(sub == planes - 1, x_high[r : r + 1], pltpu.roll(mid, planes - 1, 0))
        total += jnp.where(lane == 0, 0.0, pltpu.roll(mid, 1, 1))
        total += jnp.where(lane == width - 1, 0.0, pltpu.roll(mid, width - 1, 1))
        out_ref[r] = (mid + 0.5 * nu_ref[r // nf] * (total - 6.0 * mid)) * gas_side
    slab.wait()
    for c in copies:
        c.wait()
    selt = selt_ref[...]
    for r in range(0, rows, 2):
        both = recv[:, r * SLOTS : (r + 2) * SLOTS, :].astype(F32)
        for h in range(2):
            inc = both[:, h * SLOTS : (h + 1) * SLOTS, :].reshape(nt * SLOTS, width).astype(BF16)
            placed = lax.dot_general(
                selt, inc, (((0,), (0,)), ((), ())), preferred_element_type=F32
            )
            out_ref[r + h] = out_ref[r + h] + placed * gas_side


def local(
    flow_fields, turbulent_diffusivity, holder_unit, spray_volume_position, patch_pick_unreduced,
    droplet_motion, droplet_warmth, droplet_weightiness, droplet_multiplicity, living_spray_batches,
):
    ng, nt = lax.axis_size("grp"), lax.axis_size("tile")
    g, t = lax.axis_index("grp"), lax.axis_index("tile")
    nf, planes, rows_y, width = flow_fields.shape
    rows = nf * rows_y
    gas = jnp.where(g < ng - 1, flow_fields, 0.0)
    gas = gas.transpose(2, 0, 1, 3).reshape(rows, planes, width)
    gas_low = gas.astype(BF16)
    nu = turbulent_diffusivity.transpose(1, 0, 2)
    owner = holder_unit.reshape(planes)
    own_row = jnp.concatenate([owner, jnp.full((128 - planes,), -1, I32)]).reshape(1, 1, 128)
    slab = jax.ShapeDtypeStruct((nt, rows * SLOTS, width), BF16)
    dma = pltpu.SemaphoreType.DMA
    send, sel = pl.pallas_call(
        functools.partial(pack_kernel, nt),
        out_shape=(slab, jax.ShapeDtypeStruct((nt * SLOTS, planes), BF16)),
        in_specs=[VMEM] * 3, out_specs=(VMEM, VMEM),
        name="pack",
    )(owner.reshape(planes, 1), owner.reshape(1, planes), gas_low)
    halo_y = jax.ShapeDtypeStruct((nf, planes, width), BF16)
    halo_x = jax.ShapeDtypeStruct((rows, width), BF16)
    recv, ylo, yhi, xlo, xhi, own_all = pl.pallas_call(
        functools.partial(exchange_kernel, ng, nt, nf),
        out_shape=(slab, halo_y, halo_y, halo_x, halo_x, jax.ShapeDtypeStruct((nt, ng, 1, 128), I32)),
        in_specs=[VMEM] * 5, out_specs=(VMEM,) * 6,
        scratch_shapes=[
            dma((nt - 1,)), dma((nt - 1,)), dma((ng - 1,)), dma((ng - 1,)),
            dma((nt - 1,)), dma((nt - 1,)), dma((4,)), dma((4,)), dma((2,)),
        ],
        compiler_params=pltpu.CompilerParams(collective_id=0, has_side_effects=True),
        name="exchange",
    )(send, gas_low, gas_low[:, 0, :], gas_low[:, -1, :], own_row)
    blocks = spray_volume_position.shape[1]
    slots = nt * SLOTS
    scal = jnp.stack([g.astype(I32), t.astype(I32), living_spray_batches[0]])
    prow = blocks // 128
    dep = pl.pallas_call(
        functools.partial(parcel_kernel, ng, nt, nf),
        out_shape=slab,
        in_specs=[SMEM] + [VMEM] * 8, out_specs=VMEM,
        scratch_shapes=[
            pltpu.VMEM(((slots + 1) * 32, width), F32),
            pltpu.VMEM((slots + 1, 32, width), BF16),
            pltpu.VMEM(((slots + 1) * 32, width), F32),
            pltpu.VMEM((BATCH * 8, width), F32),
            pltpu.VMEM((6, BATCH, width), F32),
            pltpu.VMEM((BATCH * 8, width), F32),
            pltpu.VMEM((BATCH, 128, 128), BF16),
            pltpu.VMEM((prow + ng * nt, 128), I32),
            pltpu.SMEM((prow + ng * nt, 128), I32),
            pltpu.SMEM((slots + SLOTS + 1,), I32),
            pltpu.SMEM((blocks + BATCH + 8,), I32),
            dma,
        ],
        name="parcels",
    )(
        scal, recv, own_all.reshape(nt * ng, 128), patch_pick_unreduced.reshape(prow, 128),
        spray_volume_position[0], droplet_motion[0], droplet_warmth[0], droplet_weightiness[0],
        droplet_multiplicity[0],
    )
    out = pl.pallas_call(
        functools.partial(finish_kernel, ng, nt, nf),
        out_shape=jax.ShapeDtypeStruct((rows, planes, width), F32),
        in_specs=[VMEM] * 8, out_specs=VMEM,
        scratch_shapes=[
            pltpu.VMEM((nt, rows * SLOTS, width), BF16), dma((nt - 1,)), dma((nt - 1,)), dma,
        ],
        compiler_params=pltpu.CompilerParams(collective_id=1, has_side_effects=True),
        name="finish",
    )(dep, sel, gas, nu, ylo, yhi, xlo, xhi)
    return out.reshape(rows_y, nf, planes, width).transpose(1, 2, 0, 3)


def solution(mesh):
    in_specs = (
        P(None, "tile", "grp", None),
        P("tile", "grp", None),
        P("grp", "tile", None),
        P("tile", None, None),
        P("tile", None),
        P("tile", None, None, None),
        P("tile", None, None),
        P("tile", None, None),
        P("tile", None, None),
        P("tile"),
    )
    out_specs = P(None, "tile", "grp", None)
    return jax.shard_map(local, mesh=mesh, in_specs=in_specs, out_specs=out_specs, check_vma=False)
```

```python
import functools

import jax
import jax.numpy as jnp
from jax import lax
from jax.experimental import pallas as pl
from jax.experimental.pallas import tpu as pltpu
from jax.sharding import PartitionSpec as P

MESH = pl.DeviceIdType.MESH
SLOTS = 8
BATCH = 32
VMEM = pl.BlockSpec(memory_space=pltpu.VMEM)
SMEM = pl.BlockSpec(memory_space=pltpu.SMEM)
F32, BF16, I32 = jnp.float32, jnp.bfloat16, jnp.int32


def pack_kernel(ng, owners, own_ref, flow_ref, nu_ref, send_ref, sel_ref, gas_ref, low_ref, first_ref, last_ref, nut_ref):
    nf, planes, rows_y, width = flow_ref.shape
    gas_side = lax.axis_index("grp") < ng - 1
    row = jnp.broadcast_to(own_ref[0], (128, 128))
    col = row.T
    s = lax.broadcasted_iota(I32, (128, 128), 0)
    l = lax.broadcasted_iota(I32, (128, 128), 1)
    earlier = jnp.where((col == row) & (s < l), 1, 0)
    rank = jnp.sum(earlier, axis=0, keepdims=True)
    goal = (own_ref[0] * SLOTS + rank)[:, 0:planes]
    target = lax.broadcasted_iota(I32, (owners * SLOTS, planes), 0)
    sel = jnp.where(goal == target, 1.0, 0.0).astype(BF16)
    sel_ref[...] = sel
    rows = nf * rows_y
    for r in range(0, rows, 2):
        pair = []
        for q in (r, r + 1):
            cells = jnp.where(gas_side, flow_ref[q % nf, :, q // nf, :], 0.0)
            gas_ref[q] = cells
            low = cells.astype(BF16)
            low_ref[q] = low
            pair.append(jnp.dot(sel, low, preferred_element_type=F32))
        for o in range(owners):
            lo, hi = o * SLOTS, (o + 1) * SLOTS
            both = jnp.concatenate([pair[0][lo:hi], pair[1][lo:hi]], axis=0).astype(BF16)
            send_ref[o, r * SLOTS : (r + 2) * SLOTS, :] = both
    for y in range(rows_y):
        nut_ref[y] = nu_ref[:, y, :]
    first_ref[...] = gas_ref[:, 0, :].astype(BF16)
    last_ref[...] = gas_ref[:, planes - 1, :].astype(BF16)


def greet(peers):
    barrier = pltpu.get_barrier_semaphore()
    for peer in peers:
        pl.semaphore_signal(barrier, inc=1, device_id=peer, device_id_type=MESH)
    pl.semaphore_wait(barrier, len(peers))


def exchange_kernel(
    ng, nt, nf, send_ref, gas_ref, first_ref, last_ref, own_ref,
    recv_ref, ylo_ref, yhi_ref, xlo_ref, xhi_ref, all_ref,
    tile_s, tile_r, own_s, own_r, own2_s, own2_r, halo_s, halo_r, local_sem,
):
    g, t = lax.axis_index("grp"), lax.axis_index("tile")
    grp_peers = [(lax.rem(g + k, ng), t) for k in range(1, ng)]
    tile_peers = [(g, lax.rem(t + k, nt)) for k in range(1, nt)]
    greet(grp_peers + tile_peers)

    def copy(src, dst, ss, rs, dev):
        c = pltpu.make_async_remote_copy(
            src_ref=src, dst_ref=dst, send_sem=ss, recv_sem=rs, device_id=dev, device_id_type=MESH
        )
        c.start()
        return c

    own_copies = [
        copy(own_ref.at[0], all_ref.at[t, g], own_s.at[k], own_r.at[k], peer)
        for k, peer in enumerate(grp_peers)
    ]
    mine = pltpu.make_async_copy(own_ref.at[0], all_ref.at[t, g], local_sem.at[0])
    mine.start()
    slab = pltpu.make_async_copy(send_ref.at[t], recv_ref.at[t], local_sem.at[1])
    slab.start()
    rows = gas_ref.shape[0]
    others = [
        copy(gas_ref.at[pl.ds(rows - nf, nf)], ylo_ref, halo_s.at[0], halo_r.at[0], grp_peers[0]),
        copy(gas_ref.at[pl.ds(0, nf)], yhi_ref, halo_s.at[1], halo_r.at[1], grp_peers[-1]),
        copy(last_ref, xlo_ref, halo_s.at[2], halo_r.at[2], tile_peers[0]),
        copy(first_ref, xhi_ref, halo_s.at[3], halo_r.at[3], tile_peers[-1]),
    ]
    for k, peer in enumerate(tile_peers):
        others.append(copy(send_ref.at[peer[1]], recv_ref.at[t], tile_s.at[k], tile_r.at[k], peer))
    mine.wait()
    for c in own_copies:
        c.wait()
    for k, peer in enumerate(tile_peers):
        others.append(copy(all_ref.at[t], all_ref.at[t], own2_s.at[k], own2_r.at[k], peer))
    slab.wait()
    for c in others:
        c.wait()


def parcel_kernel(
    ng, nt, nf, scal_ref, recv_ref, own_ref, pick_ref, pos_ref, mot_ref, warm_ref, mass_ref, mult_ref,
    dep_ref,
    stage, table, acc, seen, par, src, hot, ints, smem, slot_of, todo, sem,
):
    g, p, live = lax.axis_index("grp"), lax.axis_index("tile"), scal_ref[0]
    slots = nt * SLOTS
    blocks = pos_ref.shape[0]
    shift = blocks.bit_length() - 1
    prow = blocks // 128
    owned = jnp.where(own_ref[...] == p, 1, 0)
    counts = jnp.sum(owned, axis=1, keepdims=True)
    which = lax.broadcasted_iota(I32, counts.shape, 0)
    counts = jnp.where(lax.rem(which, ng) < ng - 1, counts, 0)
    total = jnp.maximum(jnp.sum(counts, axis=0, keepdims=True), 1)
    pick = pick_ref[...]
    total_f = total.astype(F32)
    quotient = jnp.floor(pick.astype(F32) / total_f).astype(I32)
    left = pick - quotient * total
    left = jnp.where(left < 0, left + total, left)
    left = jnp.where(left >= total, left - total, left)
    ints[0:prow, :] = left
    ints[prow : prow + ng * nt, :] = jnp.broadcast_to(counts, (ng * nt, 128))
    to_smem = pltpu.make_async_copy(ints, smem, sem)
    to_smem.start()
    rows = recv_ref.shape[1] // SLOTS
    stage[...] = jnp.zeros_like(stage)
    for d in range(nt):
        for r in range(0, rows, 2):
            both = recv_ref[d, r * SLOTS : (r + 2) * SLOTS, :].astype(F32)
            for h in range(2):
                row = (r + h) // nf * 8 + (r + h) % nf
                stage[pl.ds(d * SLOTS * 32 + row, SLOTS, stride=32), :] = both[h * SLOTS : (h + 1) * SLOTS]

    @pl.loop(0, slots + 1)
    def _(i):
        table[i] = stage[pl.ds(pl.multiple_of(i * 32, 32), 32), :].astype(BF16)

    acc[...] = jnp.zeros_like(acc)
    src[...] = jnp.zeros_like(src)
    to_smem.wait()

    def per_device(i, carry):
        total_seen, low, high = carry
        gg, d = i // nt, lax.rem(i, nt)
        count = smem[prow + d * ng + gg, 0]
        here = gg == g

        @pl.when(here)
        def _():
            for j in range(SLOTS):
                slot_of[total_seen - low + j] = d * SLOTS + j

        after = total_seen + count
        low = jnp.where(gg < g, after, low)
        high = jnp.where(gg <= g, after, high)
        return after, low, high

    zero = jnp.int32(0)
    _, low, high = lax.fori_loop(0, (ng - 1) * nt, per_device, (zero, zero, zero))
    slot_of[slots + SLOTS] = slots

    def compact(i, n):
        for j in range(8):
            b = i * 8 + j
            k = smem[b // 128, lax.rem(b, 128)]
            todo[n] = ((k - low) << shift) + b
            n = n + jnp.where((k >= low) & (k < high) & (b < live), 1, 0)
        return n

    n = lax.fori_loop(0, (live + 7) // 8, compact, zero)
    for j in range(BATCH):
        todo[n + j] = (slots + SLOTS) << shift

    sub = lax.broadcasted_iota(I32, (128, 128), 0).astype(F32).astype(BF16)
    yes, no = jnp.ones((128, 128), BF16), jnp.zeros((128, 128), BF16)

    @pl.loop(0, (n + BATCH - 1) // BATCH)
    def _(step):
        where_at, ys = [], []
        for j in range(BATCH):
            v = todo[step * BATCH + j]
            b = v & (blocks - 1)
            slot = slot_of[v >> shift]
            cell = pos_ref[pl.ds(b, 1), :]
            y = cell >> 7
            z = (cell & 127).astype(F32).astype(BF16)
            one = jnp.where(sub == jnp.broadcast_to(z, (128, 128)), yes, no)
            hot[j] = one
            got = jnp.dot(table[slot], one, preferred_element_type=F32)
            upper = jnp.where(y < 1, got[0:8], got[8:16])
            lower = jnp.where(y < 3, got[16:24], got[24:32])
            seen[pl.ds(j * 8, 8), :] = jnp.where(y < 2, upper, lower)
            for f in range(3):
                par[f : f + 1, j, :] = mot_ref[f, pl.ds(b, 1), :]
            par[3:4, j, :] = warm_ref[pl.ds(b, 1), :]
            par[4:5, j, :] = mass_ref[pl.ds(b, 1), :]
            par[5:6, j, :] = mult_ref[pl.ds(b, 1), :]
            where_at.append(slot)
            ys.append(y)
        field = [seen[pl.ds(f, BATCH, stride=8), :] for f in range(5)]
        v0, v1, v2, warm, mass, mult = [par[f] for f in range(6)]
        r0, r1, r2 = field[0] - v0, field[1] - v1, field[2] - v2
        speed_sq = r0 * r0 + r1 * r1 + r2 * r2
        inv_surface = jnp.exp(jnp.log(mass) * (-2.0 / 3.0))
        inverse_tau = 0.8 * (1.0 + 0.15 * jnp.exp(0.3435 * jnp.log(1.0 + speed_sq))) * inv_surface
        relax = 1.0 - jnp.exp(-0.5 * inverse_tau)
        heating = 1.0 / (1.0 + jnp.exp(field[4] - field[3]))
        remain = jnp.exp(-0.3 * heating * inv_surface)
        new_mass = mass * remain
        warming = 1.0 - jnp.exp(-0.25 * inverse_tau)
        new_warm = warm + warming * (field[3] - warm) - 0.5 * (1.0 - remain)
        outs = [mass * v - new_mass * (v + relax * r) for v, r in ((v0, r0), (v1, r1), (v2, r2))]
        outs += [mass * warm - new_mass * new_warm, mass - new_mass]
        for f, o in enumerate(outs):
            src[pl.ds(f, BATCH, stride=8), :] = mult * o
        added = []
        for j in range(BATCH):
            s8 = src[pl.ds(j * 8, 8), :]
            s32 = jnp.concatenate([jnp.where(ys[j] == k, s8, 0.0) for k in range(4)], axis=0).astype(BF16)
            added.append(
                lax.dot_general(s32, hot[j], (((1,), (1,)), ((), ())), preferred_element_type=F32)
            )
        for j in range(BATCH):
            at = pl.ds(pl.multiple_of(where_at[j] * 32, 32), 32)
            acc[at, :] = acc[at, :] + added[j]

    for d in range(nt):
        for r in range(0, rows, 2):
            pair = [
                acc[pl.ds(d * SLOTS * 32 + q // nf * 8 + q % nf, SLOTS, stride=32), :] for q in (r, r + 1)
            ]
            dep_ref[d, r * SLOTS : (r + 2) * SLOTS, :] = jnp.concatenate(pair, axis=0).astype(BF16)


def finish_kernel(
    ng, nt, nf, dep_ref, selt_ref, gas_ref, nu_ref, ylo_ref, yhi_ref, xlo_ref, xhi_ref,
    out_ref, recv, part, tile_s, tile_r, local_sem,
):
    g, t = lax.axis_index("grp"), lax.axis_index("tile")
    peers = [(g, lax.rem(t + k, nt)) for k in range(1, nt)]
    greet(peers)
    copies = []
    for k, peer in enumerate(peers):
        c = pltpu.make_async_remote_copy(
            src_ref=dep_ref.at[peer[1]], dst_ref=recv.at[t], send_sem=tile_s.at[k],
            recv_sem=tile_r.at[k], device_id=peer, device_id_type=MESH,
        )
        c.start()
        copies.append(c)
    slab = pltpu.make_async_copy(dep_ref.at[t], recv.at[t], local_sem)
    slab.start()
    rows, planes, width = gas_ref.shape
    sub = lax.broadcasted_iota(I32, (planes, width), 0)
    lane = lax.broadcasted_iota(I32, (planes, width), 1)
    gas_side = jnp.where(g < ng - 1, 1.0, 0.0).astype(F32)
    has_low = jnp.where(t > 0, 1.0, 0.0).astype(F32)
    has_high = jnp.where(t < nt - 1, 1.0, 0.0).astype(F32)
    x_low = xlo_ref[...].astype(F32) * has_low
    x_high = xhi_ref[...].astype(F32) * has_high
    for r in range(rows):
        mid = gas_ref[r]
        below = gas_ref[r - nf] if r >= nf else ylo_ref[r].astype(F32)
        above = gas_ref[r + nf] if r < rows - nf else yhi_ref[r - (rows - nf)].astype(F32)
        total = below + above
        total += jnp.where(sub == 0, x_low[r : r + 1], pltpu.roll(mid, 1, 0))
        total += jnp.where(sub == planes - 1, x_high[r : r + 1], pltpu.roll(mid, planes - 1, 0))
        total += jnp.where(lane == 0, 0.0, pltpu.roll(mid, 1, 1))
        total += jnp.where(lane == width - 1, 0.0, pltpu.roll(mid, width - 1, 1))
        part[r] = (mid + 0.5 * nu_ref[r // nf] * (total - 6.0 * mid)) * gas_side
    slab.wait()
    for c in copies:
        c.wait()
    selt = selt_ref[...]
    for r in range(0, rows, 2):
        both = recv[:, r * SLOTS : (r + 2) * SLOTS, :].astype(F32)
        for h in range(2):
            inc = both[:, h * SLOTS : (h + 1) * SLOTS, :].reshape(nt * SLOTS, width).astype(BF16)
            placed = lax.dot_general(
                selt, inc, (((0,), (0,)), ((), ())), preferred_element_type=F32
            )
            q = r + h
            out_ref[q % nf, :, q // nf, :] = part[q] + placed * gas_side


def local(
    flow_fields, turbulent_diffusivity, holder_unit, spray_volume_position, patch_pick_unreduced,
    droplet_motion, droplet_warmth, droplet_weightiness, droplet_multiplicity, living_spray_batches,
):
    ng, nt = lax.axis_size("grp"), lax.axis_size("tile")
    nf, planes, rows_y, width = flow_fields.shape
    rows = nf * rows_y
    own_row = jnp.pad(holder_unit.reshape(1, 1, planes), ((0, 0), (0, 0), (0, 128 - planes)), constant_values=-1)
    slab = jax.ShapeDtypeStruct((nt, rows * SLOTS, width), BF16)
    dma = pltpu.SemaphoreType.DMA
    edge = jax.ShapeDtypeStruct((rows, width), BF16)
    send, sel, gas, gas_low, first, last, nu = pl.pallas_call(
        functools.partial(pack_kernel, ng, nt),
        out_shape=(
            slab,
            jax.ShapeDtypeStruct((nt * SLOTS, planes), BF16),
            jax.ShapeDtypeStruct((rows, planes, width), F32),
            jax.ShapeDtypeStruct((rows, planes, width), BF16),
            edge,
            edge,
            jax.ShapeDtypeStruct((rows_y, planes, width), F32),
        ),
        in_specs=[VMEM] * 3, out_specs=(VMEM,) * 7,
        name="pack",
    )(own_row, flow_fields, turbulent_diffusivity)
    halo_y = jax.ShapeDtypeStruct((nf, planes, width), BF16)
    halo_x = jax.ShapeDtypeStruct((rows, width), BF16)
    recv, ylo, yhi, xlo, xhi, own_all = pl.pallas_call(
        functools.partial(exchange_kernel, ng, nt, nf),
        out_shape=(slab, halo_y, halo_y, halo_x, halo_x, jax.ShapeDtypeStruct((nt, ng, 1, 128), I32)),
        in_specs=[VMEM] * 5, out_specs=(VMEM,) * 6,
        scratch_shapes=[
            dma((nt - 1,)), dma((nt - 1,)), dma((ng - 1,)), dma((ng - 1,)),
            dma((nt - 1,)), dma((nt - 1,)), dma((4,)), dma((4,)), dma((2,)),
        ],
        compiler_params=pltpu.CompilerParams(collective_id=0, has_side_effects=True),
        name="exchange",
    )(send, gas_low, first, last, own_row)
    blocks = spray_volume_position.shape[1]
    slots = nt * SLOTS
    prow = blocks // 128
    dep = pl.pallas_call(
        functools.partial(parcel_kernel, ng, nt, nf),
        out_shape=slab,
        in_specs=[SMEM] + [VMEM] * 8, out_specs=VMEM,
        scratch_shapes=[
            pltpu.VMEM(((slots + 1) * 32, width), F32),
            pltpu.VMEM((slots + 1, 32, width), BF16),
            pltpu.VMEM(((slots + 1) * 32, width), F32),
            pltpu.VMEM((BATCH * 8, width), F32),
            pltpu.VMEM((6, BATCH, width), F32),
            pltpu.VMEM((BATCH * 8, width), F32),
            pltpu.VMEM((BATCH, 128, 128), BF16),
            pltpu.VMEM((prow + ng * nt, 128), I32),
            pltpu.SMEM((prow + ng * nt, 128), I32),
            pltpu.SMEM((slots + SLOTS + 1,), I32),
            pltpu.SMEM((blocks + BATCH + 8,), I32),
            dma,
        ],
        name="parcels",
    )(
        living_spray_batches, recv, own_all.reshape(nt * ng, 128), patch_pick_unreduced.reshape(prow, 128),
        spray_volume_position[0], droplet_motion[0].transpose(1, 0, 2), droplet_warmth[0], droplet_weightiness[0],
        droplet_multiplicity[0],
    )
    return pl.pallas_call(
        functools.partial(finish_kernel, ng, nt, nf),
        out_shape=jax.ShapeDtypeStruct((nf, planes, rows_y, width), F32),
        in_specs=[VMEM] * 8, out_specs=VMEM,
        scratch_shapes=[
            pltpu.VMEM((nt, rows * SLOTS, width), BF16), pltpu.VMEM((rows, planes, width), F32),
            dma((nt - 1,)), dma((nt - 1,)), dma,
        ],
        compiler_params=pltpu.CompilerParams(collective_id=1, has_side_effects=True),
        name="finish",
    )(dep, sel, gas, nu, ylo, yhi, xlo, xhi)


def solution(mesh):
    in_specs = (
        P(None, "tile", "grp", None),
        P("tile", "grp", None),
        P("grp", "tile", None),
        P("tile", None, None),
        P("tile", None),
        P("tile", None, None, None),
        P("tile", None, None),
        P("tile", None, None),
        P("tile", None, None),
        P("tile"),
    )
    out_specs = P(None, "tile", "grp", None)
    return jax.shard_map(local, mesh=mesh, in_specs=in_specs, out_specs=out_specs, check_vma=False)
```

```python
import functools

import jax
import jax.numpy as jnp
from jax import lax
from jax.experimental import pallas as pl
from jax.experimental.pallas import tpu as pltpu
from jax.sharding import PartitionSpec as P

MESH = pl.DeviceIdType.MESH
SLOTS = 8
BATCH = 32
VMEM = pl.BlockSpec(memory_space=pltpu.VMEM)
SMEM = pl.BlockSpec(memory_space=pltpu.SMEM)
F32, BF16, I32 = jnp.float32, jnp.bfloat16, jnp.int32


def pack_kernel(ng, owners, own_ref, flow_ref, nu_ref, send_ref, sel_ref, gas_ref, low_ref, first_ref, last_ref, nut_ref):
    nf, planes, rows_y, width = flow_ref.shape
    gas_side = lax.axis_index("grp") < ng - 1
    row = jnp.broadcast_to(own_ref[0], (128, 128))
    col = row.T
    s = lax.broadcasted_iota(I32, (128, 128), 0)
    l = lax.broadcasted_iota(I32, (128, 128), 1)
    earlier = jnp.where((col == row) & (s < l), 1, 0)
    rank = jnp.sum(earlier, axis=0, keepdims=True)
    goal = (own_ref[0] * SLOTS + rank)[:, 0:planes]
    target = lax.broadcasted_iota(I32, (owners * SLOTS, planes), 0)
    sel = jnp.where(goal == target, 1.0, 0.0).astype(BF16)
    sel_ref[...] = sel
    rows = nf * rows_y
    for r in range(0, rows, 2):
        pair = []
        for q in (r, r + 1):
            cells = jnp.where(gas_side, flow_ref[q % nf, :, q // nf, :], 0.0)
            gas_ref[q] = cells
            low = cells.astype(BF16)
            low_ref[q] = low
            pair.append(jnp.dot(sel, low, preferred_element_type=F32))
        for o in range(owners):
            lo, hi = o * SLOTS, (o + 1) * SLOTS
            both = jnp.concatenate([pair[0][lo:hi], pair[1][lo:hi]], axis=0).astype(BF16)
            send_ref[o, r * SLOTS : (r + 2) * SLOTS, :] = both
    for y in range(rows_y):
        nut_ref[y] = nu_ref[:, y, :]
    first_ref[...] = gas_ref[:, 0, :].astype(BF16)
    last_ref[...] = gas_ref[:, planes - 1, :].astype(BF16)


def greet(peers):
    barrier = pltpu.get_barrier_semaphore()
    for peer in peers:
        pl.semaphore_signal(barrier, inc=1, device_id=peer, device_id_type=MESH)
    pl.semaphore_wait(barrier, len(peers))


def exchange_kernel(
    ng, nt, nf, send_ref, gas_ref, first_ref, last_ref, own_ref,
    recv_ref, ylo_ref, yhi_ref, xlo_ref, xhi_ref, all_ref,
    tile_s, tile_r, own_s, own_r, own2_s, own2_r, halo_s, halo_r, local_sem,
):
    g, t = lax.axis_index("grp"), lax.axis_index("tile")
    grp_peers = [(lax.rem(g + k, ng), t) for k in range(1, ng)]
    tile_peers = [(g, lax.rem(t + k, nt)) for k in range(1, nt)]
    greet(grp_peers + tile_peers)

    def copy(src, dst, ss, rs, dev):
        c = pltpu.make_async_remote_copy(
            src_ref=src, dst_ref=dst, send_sem=ss, recv_sem=rs, device_id=dev, device_id_type=MESH
        )
        c.start()
        return c

    own_copies = [
        copy(own_ref.at[0], all_ref.at[t, g], own_s.at[k], own_r.at[k], peer)
        for k, peer in enumerate(grp_peers)
    ]
    mine = pltpu.make_async_copy(own_ref.at[0], all_ref.at[t, g], local_sem.at[0])
    mine.start()
    slab = pltpu.make_async_copy(send_ref.at[t], recv_ref.at[t], local_sem.at[1])
    slab.start()
    rows = gas_ref.shape[0]
    others = [
        copy(gas_ref.at[pl.ds(rows - nf, nf)], ylo_ref, halo_s.at[0], halo_r.at[0], grp_peers[0]),
        copy(gas_ref.at[pl.ds(0, nf)], yhi_ref, halo_s.at[1], halo_r.at[1], grp_peers[-1]),
        copy(last_ref, xlo_ref, halo_s.at[2], halo_r.at[2], tile_peers[0]),
        copy(first_ref, xhi_ref, halo_s.at[3], halo_r.at[3], tile_peers[-1]),
    ]
    for k, peer in enumerate(tile_peers):
        others.append(copy(send_ref.at[peer[1]], recv_ref.at[t], tile_s.at[k], tile_r.at[k], peer))
    mine.wait()
    for c in own_copies:
        c.wait()
    for k, peer in enumerate(tile_peers):
        others.append(copy(all_ref.at[t], all_ref.at[t], own2_s.at[k], own2_r.at[k], peer))
    slab.wait()
    for c in others:
        c.wait()


def parcel_kernel(
    ng, nt, nf, scal_ref, recv_ref, own_ref, pick_ref, pos_ref, mot_ref, warm_ref, mass_ref, mult_ref,
    dep_ref,
    stage, table, acc, seen, par, src, hot, ints, smem, sem,
):
    g, p, live = lax.axis_index("grp"), lax.axis_index("tile"), scal_ref[0]
    slots = nt * SLOTS
    blocks = pos_ref.shape[0]
    shift = blocks.bit_length() - 1
    prow = blocks // 128
    owned = jnp.where(own_ref[...] == p, 1, 0)
    counts = jnp.sum(owned, axis=1, keepdims=True)
    which = lax.broadcasted_iota(I32, counts.shape, 0)
    counts = jnp.where(lax.rem(which, ng) < ng - 1, counts, 0)
    total = jnp.maximum(jnp.sum(counts, axis=0, keepdims=True), 1)
    pick = pick_ref[...]
    total_f = total.astype(F32)
    quotient = jnp.floor(pick.astype(F32) / total_f).astype(I32)
    left = pick - quotient * total
    left = jnp.where(left < 0, left + total, left)
    left = jnp.where(left >= total, left - total, left)
    group = lax.rem(which, ng)
    low = jnp.sum(jnp.where(group < g, counts, 0), axis=0, keepdims=True)
    mine = jnp.sum(jnp.where(group == g, counts, 0), axis=0, keepdims=True)
    inner = left - low
    slot = inner
    passed = jnp.zeros((1, 1), I32)
    for d in range(nt - 1):
        count = jnp.sum(jnp.where(which == d * ng + g, counts, 0), axis=0, keepdims=True)
        passed = passed + count
        slot = slot + jnp.where(inner >= passed, SLOTS - count, 0)
    row = lax.broadcasted_iota(I32, (prow, 128), 0)
    lane = lax.broadcasted_iota(I32, (prow, 128), 1)
    number = row * 128 + lane
    inside = (inner >= 0) & (inner < mine) & (number < live)
    flags = jnp.where(inside, 1, 0)
    square_a = lax.broadcasted_iota(I32, (128, 128), 0)
    square_b = lax.broadcasted_iota(I32, (128, 128), 1)
    before = jnp.where(square_a < square_b, 1.0, 0.0).astype(BF16)
    flags_low = flags.astype(F32).astype(BF16)
    place = jnp.dot(flags_low, before, preferred_element_type=F32).astype(I32)
    sums = jnp.sum(flags, axis=1, keepdims=True)
    start = jnp.zeros((1, 1), I32)
    listed = jnp.zeros((3 * prow, 128), F32)
    lane_f, slot_f = lane[0:1].astype(F32), slot.astype(F32)
    for i in range(prow):
        at = jnp.where(inside[i : i + 1], place[i : i + 1] + start, -1)
        goes = row == (at >> 7)
        parts = [
            jnp.where(goes, v, 0.0) for v in (slot_f[i : i + 1], jnp.full((1, 128), float(i), F32), lane_f)
        ]
        spot = jnp.where(square_a == (at & 127), 1.0, 0.0).astype(BF16)
        listed += lax.dot_general(
            jnp.concatenate(parts, axis=0).astype(BF16), spot, (((1,), (1,)), ((), ())),
            preferred_element_type=F32,
        )
        start = start + sums[i : i + 1]
    listed = listed.astype(I32)
    entry = (listed[0:prow] << shift) + listed[prow : 2 * prow] * 128 + listed[2 * prow :]
    ints[0:prow, :] = jnp.where(number < start, entry, slots << shift)
    ints[prow : prow + 8, :] = jnp.broadcast_to(start, (8, 128))
    to_smem = pltpu.make_async_copy(ints, smem, sem)
    to_smem.start()
    rows = recv_ref.shape[1] // SLOTS
    stage[...] = jnp.zeros_like(stage)
    for d in range(nt):
        for r in range(0, rows, 2):
            both = recv_ref[d, r * SLOTS : (r + 2) * SLOTS, :].astype(F32)
            for h in range(2):
                row = (r + h) // nf * 8 + (r + h) % nf
                stage[pl.ds(d * SLOTS * 32 + row, SLOTS, stride=32), :] = both[h * SLOTS : (h + 1) * SLOTS]

    @pl.loop(0, slots + 1)
    def _(i):
        table[i] = stage[pl.ds(pl.multiple_of(i * 32, 32), 32), :].astype(BF16)

    acc[...] = jnp.zeros_like(acc)
    src[...] = jnp.zeros_like(src)
    to_smem.wait()

    n = smem[prow, 0]
    sub = lax.broadcasted_iota(I32, (128, 128), 0).astype(F32).astype(BF16)
    yes, no = jnp.ones((128, 128), BF16), jnp.zeros((128, 128), BF16)

    @pl.loop(0, (n + BATCH - 1) // BATCH)
    def _(step):
        where_at, ys = [], []
        for j in range(BATCH):
            v = smem[step // (128 // BATCH), lax.rem(step, 128 // BATCH) * BATCH + j]
            b = v & (blocks - 1)
            slot = v >> shift
            cell = pos_ref[pl.ds(b, 1), :]
            y = cell >> 7
            z = (cell & 127).astype(F32).astype(BF16)
            one = jnp.where(sub == jnp.broadcast_to(z, (128, 128)), yes, no)
            hot[j] = one
            got = jnp.dot(table[slot], one, preferred_element_type=F32)
            upper = jnp.where(y < 1, got[0:8], got[8:16])
            lower = jnp.where(y < 3, got[16:24], got[24:32])
            seen[pl.ds(j * 8, 8), :] = jnp.where(y < 2, upper, lower)
            for f in range(3):
                par[f : f + 1, j, :] = mot_ref[f, pl.ds(b, 1), :]
            par[3:4, j, :] = warm_ref[pl.ds(b, 1), :]
            par[4:5, j, :] = mass_ref[pl.ds(b, 1), :]
            par[5:6, j, :] = mult_ref[pl.ds(b, 1), :]
            where_at.append(slot)
            ys.append(y)
        field = [seen[pl.ds(f, BATCH, stride=8), :] for f in range(5)]
        v0, v1, v2, warm, mass, mult = [par[f] for f in range(6)]
        r0, r1, r2 = field[0] - v0, field[1] - v1, field[2] - v2
        speed_sq = r0 * r0 + r1 * r1 + r2 * r2
        inv_surface = jnp.exp(jnp.log(mass) * (-2.0 / 3.0))
        inverse_tau = 0.8 * (1.0 + 0.15 * jnp.exp(0.3435 * jnp.log(1.0 + speed_sq))) * inv_surface
        relax = 1.0 - jnp.exp(-0.5 * inverse_tau)
        heating = 1.0 / (1.0 + jnp.exp(field[4] - field[3]))
        remain = jnp.exp(-0.3 * heating * inv_surface)
        new_mass = mass * remain
        warming = 1.0 - jnp.exp(-0.25 * inverse_tau)
        new_warm = warm + warming * (field[3] - warm) - 0.5 * (1.0 - remain)
        outs = [mass * v - new_mass * (v + relax * r) for v, r in ((v0, r0), (v1, r1), (v2, r2))]
        outs += [mass * warm - new_mass * new_warm, mass - new_mass]
        for f, o in enumerate(outs):
            src[pl.ds(f, BATCH, stride=8), :] = mult * o
        added = []
        for j in range(BATCH):
            s8 = src[pl.ds(j * 8, 8), :]
            s32 = jnp.concatenate([jnp.where(ys[j] == k, s8, 0.0) for k in range(4)], axis=0).astype(BF16)
            added.append(
                lax.dot_general(s32, hot[j], (((1,), (1,)), ((), ())), preferred_element_type=F32)
            )
        for j in range(BATCH):
            at = pl.ds(pl.multiple_of(where_at[j] * 32, 32), 32)
            acc[at, :] = acc[at, :] + added[j]

    for d in range(nt):
        for r in range(0, rows, 2):
            pair = [
                acc[pl.ds(d * SLOTS * 32 + q // nf * 8 + q % nf, SLOTS, stride=32), :] for q in (r, r + 1)
            ]
            dep_ref[d, r * SLOTS : (r + 2) * SLOTS, :] = jnp.concatenate(pair, axis=0).astype(BF16)


def finish_kernel(
    ng, nt, nf, dep_ref, selt_ref, gas_ref, nu_ref, ylo_ref, yhi_ref, xlo_ref, xhi_ref,
    out_ref, recv, part, tile_s, tile_r, local_sem,
):
    g, t = lax.axis_index("grp"), lax.axis_index("tile")
    peers = [(g, lax.rem(t + k, nt)) for k in range(1, nt)]
    greet(peers)
    copies = []
    for k, peer in enumerate(peers):
        c = pltpu.make_async_remote_copy(
            src_ref=dep_ref.at[peer[1]], dst_ref=recv.at[t], send_sem=tile_s.at[k],
            recv_sem=tile_r.at[k], device_id=peer, device_id_type=MESH,
        )
        c.start()
        copies.append(c)
    slab = pltpu.make_async_copy(dep_ref.at[t], recv.at[t], local_sem)
    slab.start()
    rows, planes, width = gas_ref.shape
    sub = lax.broadcasted_iota(I32, (planes, width), 0)
    lane = lax.broadcasted_iota(I32, (planes, width), 1)
    gas_side = jnp.where(g < ng - 1, 1.0, 0.0).astype(F32)
    has_low = jnp.where(t > 0, 1.0, 0.0).astype(F32)
    has_high = jnp.where(t < nt - 1, 1.0, 0.0).astype(F32)
    x_low = xlo_ref[...].astype(F32) * has_low
    x_high = xhi_ref[...].astype(F32) * has_high
    for r in range(rows):
        mid = gas_ref[r]
        below = gas_ref[r - nf] if r >= nf else ylo_ref[r].astype(F32)
        above = gas_ref[r + nf] if r < rows - nf else yhi_ref[r - (rows - nf)].astype(F32)
        total = below + above
        total += jnp.where(sub == 0, x_low[r : r + 1], pltpu.roll(mid, 1, 0))
        total += jnp.where(sub == planes - 1, x_high[r : r + 1], pltpu.roll(mid, planes - 1, 0))
        total += jnp.where(lane == 0, 0.0, pltpu.roll(mid, 1, 1))
        total += jnp.where(lane == width - 1, 0.0, pltpu.roll(mid, width - 1, 1))
        part[r] = (mid + 0.5 * nu_ref[r // nf] * (total - 6.0 * mid)) * gas_side
    slab.wait()
    for c in copies:
        c.wait()
    selt = selt_ref[...]
    for r in range(0, rows, 2):
        both = recv[:, r * SLOTS : (r + 2) * SLOTS, :].astype(F32)
        for h in range(2):
            inc = both[:, h * SLOTS : (h + 1) * SLOTS, :].reshape(nt * SLOTS, width).astype(BF16)
            placed = lax.dot_general(
                selt, inc, (((0,), (0,)), ((), ())), preferred_element_type=F32
            )
            q = r + h
            out_ref[q % nf, :, q // nf, :] = part[q] + placed * gas_side


def local(
    flow_fields, turbulent_diffusivity, holder_unit, spray_volume_position, patch_pick_unreduced,
    droplet_motion, droplet_warmth, droplet_weightiness, droplet_multiplicity, living_spray_batches,
):
    ng, nt = lax.axis_size("grp"), lax.axis_size("tile")
    nf, planes, rows_y, width = flow_fields.shape
    rows = nf * rows_y
    own_row = jnp.pad(holder_unit.reshape(1, 1, planes), ((0, 0), (0, 0), (0, 128 - planes)), constant_values=-1)
    slab = jax.ShapeDtypeStruct((nt, rows * SLOTS, width), BF16)
    slab_bytes = nt * rows * SLOTS * width * 2
    dma = pltpu.SemaphoreType.DMA
    edge = jax.ShapeDtypeStruct((rows, width), BF16)
    send, sel, gas, gas_low, first, last, nu = pl.pallas_call(
        functools.partial(pack_kernel, ng, nt),
        out_shape=(
            slab,
            jax.ShapeDtypeStruct((nt * SLOTS, planes), BF16),
            jax.ShapeDtypeStruct((rows, planes, width), F32),
            jax.ShapeDtypeStruct((rows, planes, width), BF16),
            edge,
            edge,
            jax.ShapeDtypeStruct((rows_y, planes, width), F32),
        ),
        in_specs=[VMEM] * 3, out_specs=(VMEM,) * 7,
        compiler_params=pltpu.CompilerParams(vmem_limit_bytes=slab_bytes * 2 + (6 << 20)),
        name="pack",
    )(own_row, flow_fields, turbulent_diffusivity)
    halo_y = jax.ShapeDtypeStruct((nf, planes, width), BF16)
    halo_x = jax.ShapeDtypeStruct((rows, width), BF16)
    recv, ylo, yhi, xlo, xhi, own_all = pl.pallas_call(
        functools.partial(exchange_kernel, ng, nt, nf),
        out_shape=(slab, halo_y, halo_y, halo_x, halo_x, jax.ShapeDtypeStruct((nt, ng, 1, 128), I32)),
        in_specs=[VMEM] * 5, out_specs=(VMEM,) * 6,
        scratch_shapes=[
            dma((nt - 1,)), dma((nt - 1,)), dma((ng - 1,)), dma((ng - 1,)),
            dma((nt - 1,)), dma((nt - 1,)), dma((4,)), dma((4,)), dma((2,)),
        ],
        compiler_params=pltpu.CompilerParams(collective_id=0, has_side_effects=True, vmem_limit_bytes=slab_bytes * 2 + (6 << 20)),
        name="exchange",
    )(send, gas_low, first, last, own_row)
    blocks = spray_volume_position.shape[1]
    slots = nt * SLOTS
    prow = blocks // 128
    dep = pl.pallas_call(
        functools.partial(parcel_kernel, ng, nt, nf),
        out_shape=slab,
        in_specs=[SMEM] + [VMEM] * 8, out_specs=VMEM,
        scratch_shapes=[
            pltpu.VMEM(((slots + 1) * 32, width), F32),
            pltpu.VMEM((slots + 1, 32, width), BF16),
            pltpu.VMEM(((slots + 1) * 32, width), F32),
            pltpu.VMEM((BATCH * 8, width), F32),
            pltpu.VMEM((6, BATCH, width), F32),
            pltpu.VMEM((BATCH * 8, width), F32),
            pltpu.VMEM((BATCH, 128, 128), BF16),
            pltpu.VMEM((prow + 8, 128), I32),
            pltpu.SMEM((prow + 8, 128), I32),
            dma,
        ],
        compiler_params=pltpu.CompilerParams(vmem_limit_bytes=slab_bytes * 12 + (8 << 20)),
        name="parcels",
    )(
        living_spray_batches, recv, own_all.reshape(nt * ng, 128), patch_pick_unreduced.reshape(prow, 128),
        spray_volume_position[0], droplet_motion[0].transpose(1, 0, 2), droplet_warmth[0], droplet_weightiness[0],
        droplet_multiplicity[0],
    )
    return pl.pallas_call(
        functools.partial(finish_kernel, ng, nt, nf),
        out_shape=jax.ShapeDtypeStruct((nf, planes, rows_y, width), F32),
        in_specs=[VMEM] * 8, out_specs=VMEM,
        scratch_shapes=[
            pltpu.VMEM((nt, rows * SLOTS, width), BF16), pltpu.VMEM((rows, planes, width), F32),
            dma((nt - 1,)), dma((nt - 1,)), dma,
        ],
        compiler_params=pltpu.CompilerParams(collective_id=1, has_side_effects=True, vmem_limit_bytes=slab_bytes * 2 + (6 << 20)),
        name="finish",
    )(dep, sel, gas, nu, ylo, yhi, xlo, xhi)


def solution(mesh):
    in_specs = (
        P(None, "tile", "grp", None),
        P("tile", "grp", None),
        P("grp", "tile", None),
        P("tile", None, None),
        P("tile", None),
        P("tile", None, None, None),
        P("tile", None, None),
        P("tile", None, None),
        P("tile", None, None),
        P("tile"),
    )
    out_specs = P(None, "tile", "grp", None)
    return jax.shard_map(local, mesh=mesh, in_specs=in_specs, out_specs=out_specs, check_vma=False)
```

```python
import functools

import jax
import jax.numpy as jnp
from jax import lax
from jax.experimental import pallas as pl
from jax.experimental.pallas import tpu as pltpu
from jax.sharding import PartitionSpec as P

MESH = pl.DeviceIdType.MESH
SLOTS = 8
BATCH = 32
HBM = pl.BlockSpec(memory_space=pltpu.MemorySpace.HBM)
VMEM = pl.BlockSpec(memory_space=pltpu.VMEM)
SMEM = pl.BlockSpec(memory_space=pltpu.SMEM)
F32, BF16, I32 = jnp.float32, jnp.bfloat16, jnp.int32


def pack_kernel(ng, owners, holder_ref, flow_ref, send_ref, sel_ref, gas_ref, low_ref, first_ref, last_ref, padded_ref):
    nf, planes, rows_y, width = flow_ref.shape
    gas_side = lax.axis_index("grp") < ng - 1
    padded_ref[0] = jnp.full((1, 128), -1, I32)
    padded_ref[0, :, 0:planes] = holder_ref[...]
    own = padded_ref[0]
    row = jnp.broadcast_to(own, (128, 128))
    col = row.T
    s = lax.broadcasted_iota(I32, (128, 128), 0)
    l = lax.broadcasted_iota(I32, (128, 128), 1)
    earlier = jnp.where((col == row) & (s < l), 1, 0)
    rank = jnp.sum(earlier, axis=0, keepdims=True)
    goal = (own * SLOTS + rank)[:, 0:planes]
    target = lax.broadcasted_iota(I32, (owners * SLOTS, planes), 0)
    sel = jnp.where(goal == target, 1.0, 0.0).astype(BF16)
    sel_ref[...] = sel
    rows = nf * rows_y
    for r in range(0, rows, 2):
        pair = []
        for q in (r, r + 1):
            cells = jnp.where(gas_side, flow_ref[q % nf, :, q // nf, :], 0.0)
            gas_ref[q] = cells
            low = cells.astype(BF16)
            low_ref[q] = low
            pair.append(jnp.dot(sel, low, preferred_element_type=F32))
        for o in range(owners):
            lo, hi = o * SLOTS, (o + 1) * SLOTS
            both = jnp.concatenate([pair[0][lo:hi], pair[1][lo:hi]], axis=0).astype(BF16)
            send_ref[o, r * SLOTS : (r + 2) * SLOTS, :] = both
    first_ref[...] = gas_ref[:, 0, :].astype(BF16)
    last_ref[...] = gas_ref[:, planes - 1, :].astype(BF16)


def greet(peers):
    barrier = pltpu.get_barrier_semaphore()
    for peer in peers:
        pl.semaphore_signal(barrier, inc=1, device_id=peer, device_id_type=MESH)
    pl.semaphore_wait(barrier, len(peers))


def exchange_kernel(
    ng, nt, nf, send_ref, gas_ref, first_ref, last_ref, own_ref,
    recv_ref, ylo_ref, yhi_ref, xlo_ref, xhi_ref, all_ref,
    tile_s, tile_r, own_s, own_r, own2_s, own2_r, halo_s, halo_r, local_sem,
):
    g, t = lax.axis_index("grp"), lax.axis_index("tile")
    grp_peers = [(lax.rem(g + k, ng), t) for k in range(1, ng)]
    tile_peers = [(g, lax.rem(t + k, nt)) for k in range(1, nt)]
    greet(grp_peers + tile_peers)

    def copy(src, dst, ss, rs, dev):
        c = pltpu.make_async_remote_copy(
            src_ref=src, dst_ref=dst, send_sem=ss, recv_sem=rs, device_id=dev, device_id_type=MESH
        )
        c.start()
        return c

    own_copies = [
        copy(own_ref.at[0], all_ref.at[t, g], own_s.at[k], own_r.at[k], peer)
        for k, peer in enumerate(grp_peers)
    ]
    mine = pltpu.make_async_copy(own_ref.at[0], all_ref.at[t, g], local_sem.at[0])
    mine.start()
    slab = pltpu.make_async_copy(send_ref.at[t], recv_ref.at[t], local_sem.at[1])
    slab.start()
    rows = gas_ref.shape[0]
    others = [
        copy(gas_ref.at[pl.ds(rows - nf, nf)], ylo_ref, halo_s.at[0], halo_r.at[0], grp_peers[0]),
        copy(gas_ref.at[pl.ds(0, nf)], yhi_ref, halo_s.at[1], halo_r.at[1], grp_peers[-1]),
        copy(last_ref, xlo_ref, halo_s.at[2], halo_r.at[2], tile_peers[0]),
        copy(first_ref, xhi_ref, halo_s.at[3], halo_r.at[3], tile_peers[-1]),
    ]
    for k, peer in enumerate(tile_peers):
        others.append(copy(send_ref.at[peer[1]], recv_ref.at[t], tile_s.at[k], tile_r.at[k], peer))
    mine.wait()
    for c in own_copies:
        c.wait()
    for k, peer in enumerate(tile_peers):
        others.append(copy(all_ref.at[t], all_ref.at[t], own2_s.at[k], own2_r.at[k], peer))
    slab.wait()
    for c in others:
        c.wait()


def parcel_kernel(
    ng, nt, nf, scal_ref, recv_ref, own_ref, pick_ref, pos_hbm, mot_hbm, warm_hbm, mass_hbm, mult_hbm,
    dep_ref,
    pos_ref, mot_ref, warm_ref, mass_ref, mult_ref, load_sem, stage, table, acc, seen, par, src, hot, ints, smem, sem,
):
    g, p, live = lax.axis_index("grp"), lax.axis_index("tile"), scal_ref[0]
    pairs = [(pos_hbm, pos_ref), (warm_hbm, warm_ref), (mass_hbm, mass_ref), (mult_hbm, mult_ref)]
    pairs += [(mot_hbm.at[f], mot_ref.at[f]) for f in range(3)]
    loads = [pltpu.make_async_copy(a, b, load_sem.at[k]) for k, (a, b) in enumerate(pairs)]
    for c in loads:
        c.start()
    slots = nt * SLOTS
    blocks = pos_ref.shape[0]
    shift = blocks.bit_length() - 1
    prow = blocks // 128
    owned = jnp.where(own_ref[...] == p, 1, 0)
    counts = jnp.sum(owned, axis=1, keepdims=True)
    which = lax.broadcasted_iota(I32, counts.shape, 0)
    counts = jnp.where(lax.rem(which, ng) < ng - 1, counts, 0)
    total = jnp.maximum(jnp.sum(counts, axis=0, keepdims=True), 1)
    pick = pick_ref[...]
    total_f = total.astype(F32)
    quotient = jnp.floor(pick.astype(F32) / total_f).astype(I32)
    left = pick - quotient * total
    left = jnp.where(left < 0, left + total, left)
    left = jnp.where(left >= total, left - total, left)
    group = lax.rem(which, ng)
    low = jnp.sum(jnp.where(group < g, counts, 0), axis=0, keepdims=True)
    mine = jnp.sum(jnp.where(group == g, counts, 0), axis=0, keepdims=True)
    inner = left - low
    slot = inner
    passed = jnp.zeros((1, 1), I32)
    for d in range(nt - 1):
        count = jnp.sum(jnp.where(which == d * ng + g, counts, 0), axis=0, keepdims=True)
        passed = passed + count
        slot = slot + jnp.where(inner >= passed, SLOTS - count, 0)
    row = lax.broadcasted_iota(I32, (prow, 128), 0)
    lane = lax.broadcasted_iota(I32, (prow, 128), 1)
    number = row * 128 + lane
    inside = (inner >= 0) & (inner < mine) & (number < live)
    flags = jnp.where(inside, 1, 0)
    square_a = lax.broadcasted_iota(I32, (128, 128), 0)
    square_b = lax.broadcasted_iota(I32, (128, 128), 1)
    before = jnp.where(square_a < square_b, 1.0, 0.0).astype(BF16)
    flags_low = flags.astype(F32).astype(BF16)
    place = jnp.dot(flags_low, before, preferred_element_type=F32).astype(I32)
    sums = jnp.sum(flags, axis=1, keepdims=True)
    start = jnp.zeros((1, 1), I32)
    listed = jnp.zeros((3 * prow, 128), F32)
    lane_f, slot_f = lane[0:1].astype(F32), slot.astype(F32)
    for i in range(prow):
        at = jnp.where(inside[i : i + 1], place[i : i + 1] + start, -1)
        goes = row == (at >> 7)
        parts = [
            jnp.where(goes, v, 0.0) for v in (slot_f[i : i + 1], jnp.full((1, 128), float(i), F32), lane_f)
        ]
        spot = jnp.where(square_a == (at & 127), 1.0, 0.0).astype(BF16)
        listed += lax.dot_general(
            jnp.concatenate(parts, axis=0).astype(BF16), spot, (((1,), (1,)), ((), ())),
            preferred_element_type=F32,
        )
        start = start + sums[i : i + 1]
    listed = listed.astype(I32)
    entry = (listed[0:prow] << shift) + listed[prow : 2 * prow] * 128 + listed[2 * prow :]
    ints[0:prow, :] = jnp.where(number < start, entry, slots << shift)
    ints[prow : prow + 8, :] = jnp.broadcast_to(start, (8, 128))
    to_smem = pltpu.make_async_copy(ints, smem, sem)
    to_smem.start()
    rows = recv_ref.shape[1] // SLOTS
    stage[...] = jnp.zeros_like(stage)
    for d in range(nt):
        for r in range(0, rows, 2):
            both = recv_ref[d, r * SLOTS : (r + 2) * SLOTS, :].astype(F32)
            for h in range(2):
                row = (r + h) // nf * 8 + (r + h) % nf
                stage[pl.ds(d * SLOTS * 32 + row, SLOTS, stride=32), :] = both[h * SLOTS : (h + 1) * SLOTS]

    @pl.loop(0, slots + 1)
    def _(i):
        table[i] = stage[pl.ds(pl.multiple_of(i * 32, 32), 32), :].astype(BF16)

    acc[...] = jnp.zeros_like(acc)
    src[...] = jnp.zeros_like(src)
    to_smem.wait()

    n = smem[prow, 0]
    for c in loads:
        c.wait()
    sub = lax.broadcasted_iota(I32, (128, 128), 0).astype(F32).astype(BF16)
    yes, no = jnp.ones((128, 128), BF16), jnp.zeros((128, 128), BF16)

    @pl.loop(0, (n + BATCH - 1) // BATCH)
    def _(step):
        where_at, ys = [], []
        for j in range(BATCH):
            v = smem[step // (128 // BATCH), lax.rem(step, 128 // BATCH) * BATCH + j]
            b = v & (blocks - 1)
            slot = v >> shift
            cell = pos_ref[pl.ds(b, 1), :]
            y = cell >> 7
            z = (cell & 127).astype(F32).astype(BF16)
            one = jnp.where(sub == jnp.broadcast_to(z, (128, 128)), yes, no)
            hot[j] = one
            got = jnp.dot(table[slot], one, preferred_element_type=F32)
            upper = jnp.where(y < 1, got[0:8], got[8:16])
            lower = jnp.where(y < 3, got[16:24], got[24:32])
            seen[pl.ds(j * 8, 8), :] = jnp.where(y < 2, upper, lower)
            for f in range(3):
                par[f : f + 1, j, :] = mot_ref[f, pl.ds(b, 1), :]
            par[3:4, j, :] = warm_ref[pl.ds(b, 1), :]
            par[4:5, j, :] = mass_ref[pl.ds(b, 1), :]
            par[5:6, j, :] = mult_ref[pl.ds(b, 1), :]
            where_at.append(slot)
            ys.append(y)
        field = [seen[pl.ds(f, BATCH, stride=8), :] for f in range(5)]
        v0, v1, v2, warm, mass, mult = [par[f] for f in range(6)]
        r0, r1, r2 = field[0] - v0, field[1] - v1, field[2] - v2
        speed_sq = r0 * r0 + r1 * r1 + r2 * r2
        inv_surface = jnp.exp(jnp.log(mass) * (-2.0 / 3.0))
        inverse_tau = 0.8 * (1.0 + 0.15 * jnp.exp(0.3435 * jnp.log(1.0 + speed_sq))) * inv_surface
        relax = 1.0 - jnp.exp(-0.5 * inverse_tau)
        heating = 1.0 / (1.0 + jnp.exp(field[4] - field[3]))
        remain = jnp.exp(-0.3 * heating * inv_surface)
        new_mass = mass * remain
        warming = 1.0 - jnp.exp(-0.25 * inverse_tau)
        new_warm = warm + warming * (field[3] - warm) - 0.5 * (1.0 - remain)
        outs = [mass * v - new_mass * (v + relax * r) for v, r in ((v0, r0), (v1, r1), (v2, r2))]
        outs += [mass * warm - new_mass * new_warm, mass - new_mass]
        for f, o in enumerate(outs):
            src[pl.ds(f, BATCH, stride=8), :] = mult * o
        added = []
        for j in range(BATCH):
            s8 = src[pl.ds(j * 8, 8), :]
            s32 = jnp.concatenate([jnp.where(ys[j] == k, s8, 0.0) for k in range(4)], axis=0).astype(BF16)
            added.append(
                lax.dot_general(s32, hot[j], (((1,), (1,)), ((), ())), preferred_element_type=F32)
            )
        for j in range(BATCH):
            at = pl.ds(pl.multiple_of(where_at[j] * 32, 32), 32)
            acc[at, :] = acc[at, :] + added[j]

    for d in range(nt):
        for r in range(0, rows, 2):
            pair = [
                acc[pl.ds(d * SLOTS * 32 + q // nf * 8 + q % nf, SLOTS, stride=32), :] for q in (r, r + 1)
            ]
            dep_ref[d, r * SLOTS : (r + 2) * SLOTS, :] = jnp.concatenate(pair, axis=0).astype(BF16)


def finish_kernel(
    ng, nt, nf, dep_ref, selt_ref, gas_ref, nu_ref, ylo_ref, yhi_ref, xlo_ref, xhi_ref,
    out_ref, recv, part, tile_s, tile_r, local_sem,
):
    g, t = lax.axis_index("grp"), lax.axis_index("tile")
    peers = [(g, lax.rem(t + k, nt)) for k in range(1, nt)]
    greet(peers)
    copies = []
    for k, peer in enumerate(peers):
        c = pltpu.make_async_remote_copy(
            src_ref=dep_ref.at[peer[1]], dst_ref=recv.at[t], send_sem=tile_s.at[k],
            recv_sem=tile_r.at[k], device_id=peer, device_id_type=MESH,
        )
        c.start()
        copies.append(c)
    slab = pltpu.make_async_copy(dep_ref.at[t], recv.at[t], local_sem)
    slab.start()
    rows, planes, width = gas_ref.shape
    sub = lax.broadcasted_iota(I32, (planes, width), 0)
    lane = lax.broadcasted_iota(I32, (planes, width), 1)
    gas_side = jnp.where(g < ng - 1, 1.0, 0.0).astype(F32)
    has_low = jnp.where(t > 0, 1.0, 0.0).astype(F32)
    has_high = jnp.where(t < nt - 1, 1.0, 0.0).astype(F32)
    x_low = xlo_ref[...].astype(F32) * has_low
    x_high = xhi_ref[...].astype(F32) * has_high
    for r in range(rows):
        mid = gas_ref[r]
        below = gas_ref[r - nf] if r >= nf else ylo_ref[r].astype(F32)
        above = gas_ref[r + nf] if r < rows - nf else yhi_ref[r - (rows - nf)].astype(F32)
        total = below + above
        total += jnp.where(sub == 0, x_low[r : r + 1], pltpu.roll(mid, 1, 0))
        total += jnp.where(sub == planes - 1, x_high[r : r + 1], pltpu.roll(mid, planes - 1, 0))
        total += jnp.where(lane == 0, 0.0, pltpu.roll(mid, 1, 1))
        total += jnp.where(lane == width - 1, 0.0, pltpu.roll(mid, width - 1, 1))
        part[r] = (mid + 0.5 * nu_ref[:, r // nf, :] * (total - 6.0 * mid)) * gas_side
    slab.wait()
    for c in copies:
        c.wait()
    selt = selt_ref[...]
    for r in range(0, rows, 2):
        both = recv[:, r * SLOTS : (r + 2) * SLOTS, :].astype(F32)
        for h in range(2):
            inc = both[:, h * SLOTS : (h + 1) * SLOTS, :].reshape(nt * SLOTS, width).astype(BF16)
            placed = lax.dot_general(
                selt, inc, (((0,), (0,)), ((), ())), preferred_element_type=F32
            )
            q = r + h
            out_ref[q % nf, :, q // nf, :] = part[q] + placed * gas_side


def local(
    flow_fields, turbulent_diffusivity, holder_unit, spray_volume_position, patch_pick_unreduced,
    droplet_motion, droplet_warmth, droplet_weightiness, droplet_multiplicity, living_spray_batches,
):
    ng, nt = lax.axis_size("grp"), lax.axis_size("tile")
    nf, planes, rows_y, width = flow_fields.shape
    rows = nf * rows_y
    slab = jax.ShapeDtypeStruct((nt, rows * SLOTS, width), BF16)
    slab_bytes = nt * rows * SLOTS * width * 2
    dma = pltpu.SemaphoreType.DMA
    edge = jax.ShapeDtypeStruct((rows, width), BF16)
    send, sel, gas, gas_low, first, last, own_row = pl.pallas_call(
        functools.partial(pack_kernel, ng, nt),
        out_shape=(
            slab,
            jax.ShapeDtypeStruct((nt * SLOTS, planes), BF16),
            jax.ShapeDtypeStruct((rows, planes, width), F32),
            jax.ShapeDtypeStruct((rows, planes, width), BF16),
            edge,
            edge,
            jax.ShapeDtypeStruct((1, 1, 128), I32),
        ),
        in_specs=[VMEM] * 2, out_specs=(VMEM,) * 7,
        compiler_params=pltpu.CompilerParams(vmem_limit_bytes=slab_bytes * 2 + (6 << 20)),
        name="pack",
    )(holder_unit.reshape(1, planes), flow_fields)
    halo_y = jax.ShapeDtypeStruct((nf, planes, width), BF16)
    halo_x = jax.ShapeDtypeStruct((rows, width), BF16)
    blocks = spray_volume_position.shape[1]
    slots = nt * SLOTS
    prow = blocks // 128
    bulk = (
        patch_pick_unreduced.reshape(prow, 128), spray_volume_position[0],
        droplet_motion[0].transpose(1, 0, 2), droplet_warmth[0], droplet_weightiness[0],
        droplet_multiplicity[0],
    )
    recv, ylo, yhi, xlo, xhi, own_all = pl.pallas_call(
        functools.partial(exchange_kernel, ng, nt, nf),
        out_shape=(slab, halo_y, halo_y, halo_x, halo_x, jax.ShapeDtypeStruct((nt, ng, 1, 128), I32)),
        in_specs=[VMEM] * 5, out_specs=(VMEM,) * 6,
        scratch_shapes=[
            dma((nt - 1,)), dma((nt - 1,)), dma((ng - 1,)), dma((ng - 1,)),
            dma((nt - 1,)), dma((nt - 1,)), dma((4,)), dma((4,)), dma((2,)),
        ],
        compiler_params=pltpu.CompilerParams(collective_id=0, has_side_effects=True, vmem_limit_bytes=slab_bytes * 2 + (6 << 20)),
        name="exchange",
    )(send, gas_low, first, last, own_row)
    dep = pl.pallas_call(
        functools.partial(parcel_kernel, ng, nt, nf),
        out_shape=slab,
        in_specs=[SMEM] + [VMEM] * 3 + [HBM] * 5, out_specs=VMEM,
        scratch_shapes=[
            pltpu.VMEM((blocks, 128), I32),
            pltpu.VMEM((3, blocks, 128), F32),
            pltpu.VMEM((blocks, 128), F32),
            pltpu.VMEM((blocks, 128), F32),
            pltpu.VMEM((blocks, 128), F32),
            dma((7,)),
            pltpu.VMEM(((slots + 1) * 32, width), F32),
            pltpu.VMEM((slots + 1, 32, width), BF16),
            pltpu.VMEM(((slots + 1) * 32, width), F32),
            pltpu.VMEM((BATCH * 8, width), F32),
            pltpu.VMEM((6, BATCH, width), F32),
            pltpu.VMEM((BATCH * 8, width), F32),
            pltpu.VMEM((BATCH, 128, 128), BF16),
            pltpu.VMEM((prow + 8, 128), I32),
            pltpu.SMEM((prow + 8, 128), I32),
            dma,
        ],
        compiler_params=pltpu.CompilerParams(vmem_limit_bytes=63_900_000),
        name="parcels",
    )(
        living_spray_batches, recv, own_all.reshape(nt * ng, 128), *bulk,
    )
    return pl.pallas_call(
        functools.partial(finish_kernel, ng, nt, nf),
        out_shape=jax.ShapeDtypeStruct((nf, planes, rows_y, width), F32),
        in_specs=[VMEM] * 8, out_specs=VMEM,
        scratch_shapes=[
            pltpu.VMEM((nt, rows * SLOTS, width), BF16), pltpu.VMEM((rows, planes, width), F32),
            dma((nt - 1,)), dma((nt - 1,)), dma,
        ],
        compiler_params=pltpu.CompilerParams(collective_id=1, has_side_effects=True, vmem_limit_bytes=slab_bytes * 2 + (6 << 20)),
        name="finish",
    )(dep, sel, gas, turbulent_diffusivity, ylo, yhi, xlo, xhi)


def solution(mesh):
    in_specs = (
        P(None, "tile", "grp", None),
        P("tile", "grp", None),
        P("grp", "tile", None),
        P("tile", None, None),
        P("tile", None),
        P("tile", None, None, None),
        P("tile", None, None),
        P("tile", None, None),
        P("tile", None, None),
        P("tile"),
    )
    out_specs = P(None, "tile", "grp", None)
    return jax.shard_map(local, mesh=mesh, in_specs=in_specs, out_specs=out_specs, check_vma=False)
```

```python
import functools

import jax
import jax.numpy as jnp
from jax import lax
from jax.experimental import pallas as pl
from jax.experimental.pallas import tpu as pltpu
from jax.sharding import PartitionSpec as P

MESH = pl.DeviceIdType.MESH
SLOTS = 8
BATCH = 64
HBM = pl.BlockSpec(memory_space=pltpu.MemorySpace.HBM)
VMEM = pl.BlockSpec(memory_space=pltpu.VMEM)
SMEM = pl.BlockSpec(memory_space=pltpu.SMEM)
F32, BF16, I32 = jnp.float32, jnp.bfloat16, jnp.int32


def pack_kernel(ng, owners, holder_ref, flow_ref, send_ref, sel_ref, gas_ref, low_ref, first_ref, last_ref, padded_ref):
    nf, planes, rows_y, width = flow_ref.shape
    gas_side = lax.axis_index("grp") < ng - 1
    padded_ref[0] = jnp.full((1, 128), -1, I32)
    padded_ref[0, :, 0:planes] = holder_ref[...]
    own = padded_ref[0]
    row = jnp.broadcast_to(own, (128, 128))
    col = row.T
    s = lax.broadcasted_iota(I32, (128, 128), 0)
    l = lax.broadcasted_iota(I32, (128, 128), 1)
    earlier = jnp.where((col == row) & (s < l), 1, 0)
    rank = jnp.sum(earlier, axis=0, keepdims=True)
    goal = (own * SLOTS + rank)[:, 0:planes]
    target = lax.broadcasted_iota(I32, (owners * SLOTS, planes), 0)
    sel = jnp.where(goal == target, 1.0, 0.0).astype(BF16)
    sel_ref[...] = sel
    rows = nf * rows_y
    for r in range(0, rows, 2):
        pair = []
        for q in (r, r + 1):
            cells = jnp.where(gas_side, flow_ref[q % nf, :, q // nf, :], 0.0)
            gas_ref[q] = cells
            low = cells.astype(BF16)
            low_ref[q] = low
            pair.append(jnp.dot(sel, low, preferred_element_type=F32))
        for o in range(owners):
            lo, hi = o * SLOTS, (o + 1) * SLOTS
            both = jnp.concatenate([pair[0][lo:hi], pair[1][lo:hi]], axis=0).astype(BF16)
            send_ref[o, r * SLOTS : (r + 2) * SLOTS, :] = both
    first_ref[...] = gas_ref[:, 0, :].astype(BF16)
    last_ref[...] = gas_ref[:, planes - 1, :].astype(BF16)


def greet(peers):
    barrier = pltpu.get_barrier_semaphore()
    for peer in peers:
        pl.semaphore_signal(barrier, inc=1, device_id=peer, device_id_type=MESH)
    pl.semaphore_wait(barrier, len(peers))


def exchange_kernel(
    ng, nt, nf, send_ref, gas_ref, first_ref, last_ref, own_ref,
    recv_ref, ylo_ref, yhi_ref, xlo_ref, xhi_ref, all_ref,
    tile_s, tile_r, own_s, own_r, own2_s, own2_r, halo_s, halo_r, local_sem,
):
    g, t = lax.axis_index("grp"), lax.axis_index("tile")
    grp_peers = [(lax.rem(g + k, ng), t) for k in range(1, ng)]
    tile_peers = [(g, lax.rem(t + k, nt)) for k in range(1, nt)]
    greet(grp_peers + tile_peers)

    def copy(src, dst, ss, rs, dev):
        c = pltpu.make_async_remote_copy(
            src_ref=src, dst_ref=dst, send_sem=ss, recv_sem=rs, device_id=dev, device_id_type=MESH
        )
        c.start()
        return c

    own_copies = [
        copy(own_ref.at[0], all_ref.at[t, g], own_s.at[k], own_r.at[k], peer)
        for k, peer in enumerate(grp_peers)
    ]
    mine = pltpu.make_async_copy(own_ref.at[0], all_ref.at[t, g], local_sem.at[0])
    mine.start()
    slab = pltpu.make_async_copy(send_ref.at[t], recv_ref.at[t], local_sem.at[1])
    slab.start()
    rows = gas_ref.shape[0]
    others = [
        copy(gas_ref.at[pl.ds(rows - nf, nf)], ylo_ref, halo_s.at[0], halo_r.at[0], grp_peers[0]),
        copy(gas_ref.at[pl.ds(0, nf)], yhi_ref, halo_s.at[1], halo_r.at[1], grp_peers[-1]),
        copy(last_ref, xlo_ref, halo_s.at[2], halo_r.at[2], tile_peers[0]),
        copy(first_ref, xhi_ref, halo_s.at[3], halo_r.at[3], tile_peers[-1]),
    ]
    for k, peer in enumerate(tile_peers):
        others.append(copy(send_ref.at[peer[1]], recv_ref.at[t], tile_s.at[k], tile_r.at[k], peer))
    mine.wait()
    for c in own_copies:
        c.wait()
    for k, peer in enumerate(tile_peers):
        others.append(copy(all_ref.at[t], all_ref.at[t], own2_s.at[k], own2_r.at[k], peer))
    slab.wait()
    for c in others:
        c.wait()


def parcel_kernel(
    ng, nt, nf, scal_ref, recv_ref, own_ref, pick_ref, pos_hbm, mot_hbm, warm_hbm, mass_hbm, mult_hbm,
    dep_ref,
    pos_ref, mot_ref, warm_ref, mass_ref, mult_ref, load_sem, stage, table, acc, seen, par, src, hot, ints, smem, sem,
):
    g, p, live = lax.axis_index("grp"), lax.axis_index("tile"), scal_ref[0]
    pairs = [(pos_hbm, pos_ref), (warm_hbm, warm_ref), (mass_hbm, mass_ref), (mult_hbm, mult_ref)]
    pairs += [(mot_hbm.at[f], mot_ref.at[f]) for f in range(3)]
    loads = [pltpu.make_async_copy(a, b, load_sem.at[k]) for k, (a, b) in enumerate(pairs)]
    for c in loads:
        c.start()
    slots = nt * SLOTS
    blocks = pos_ref.shape[0]
    shift = blocks.bit_length() - 1
    prow = blocks // 128
    owned = jnp.where(own_ref[...] == p, 1, 0)
    counts = jnp.sum(owned, axis=1, keepdims=True)
    which = lax.broadcasted_iota(I32, counts.shape, 0)
    counts = jnp.where(lax.rem(which, ng) < ng - 1, counts, 0)
    total = jnp.maximum(jnp.sum(counts, axis=0, keepdims=True), 1)
    pick = pick_ref[...]
    total_f = total.astype(F32)
    quotient = jnp.floor(pick.astype(F32) / total_f).astype(I32)
    left = pick - quotient * total
    left = jnp.where(left < 0, left + total, left)
    left = jnp.where(left >= total, left - total, left)
    group = lax.rem(which, ng)
    low = jnp.sum(jnp.where(group < g, counts, 0), axis=0, keepdims=True)
    mine = jnp.sum(jnp.where(group == g, counts, 0), axis=0, keepdims=True)
    inner = left - low
    slot = inner
    passed = jnp.zeros((1, 1), I32)
    for d in range(nt - 1):
        count = jnp.sum(jnp.where(which == d * ng + g, counts, 0), axis=0, keepdims=True)
        passed = passed + count
        slot = slot + jnp.where(inner >= passed, SLOTS - count, 0)
    row = lax.broadcasted_iota(I32, (prow, 128), 0)
    lane = lax.broadcasted_iota(I32, (prow, 128), 1)
    number = row * 128 + lane
    inside = (inner >= 0) & (inner < mine) & (number < live)
    flags = jnp.where(inside, 1, 0)
    square_a = lax.broadcasted_iota(I32, (128, 128), 0)
    square_b = lax.broadcasted_iota(I32, (128, 128), 1)
    before = jnp.where(square_a < square_b, 1.0, 0.0).astype(BF16)
    flags_low = flags.astype(F32).astype(BF16)
    place = jnp.dot(flags_low, before, preferred_element_type=F32).astype(I32)
    sums = jnp.sum(flags, axis=1, keepdims=True)
    start = jnp.zeros((1, 1), I32)
    listed = jnp.zeros((3 * prow, 128), F32)
    lane_f, slot_f = lane[0:1].astype(F32), slot.astype(F32)
    for i in range(prow):
        at = jnp.where(inside[i : i + 1], place[i : i + 1] + start, -1)
        goes = row == (at >> 7)
        parts = [
            jnp.where(goes, v, 0.0) for v in (slot_f[i : i + 1], jnp.full((1, 128), float(i), F32), lane_f)
        ]
        spot = jnp.where(square_a == (at & 127), 1.0, 0.0).astype(BF16)
        listed += lax.dot_general(
            jnp.concatenate(parts, axis=0).astype(BF16), spot, (((1,), (1,)), ((), ())),
            preferred_element_type=F32,
        )
        start = start + sums[i : i + 1]
    listed = listed.astype(I32)
    entry = (listed[0:prow] << shift) + listed[prow : 2 * prow] * 128 + listed[2 * prow :]
    ints[0:prow, :] = jnp.where(number < start, entry, slots << shift)
    ints[prow : prow + 8, :] = jnp.broadcast_to(start, (8, 128))
    to_smem = pltpu.make_async_copy(ints, smem, sem)
    to_smem.start()
    rows = recv_ref.shape[1] // SLOTS
    stage[...] = jnp.zeros_like(stage)
    for d in range(nt):
        for r in range(0, rows, 2):
            both = recv_ref[d, r * SLOTS : (r + 2) * SLOTS, :].astype(F32)
            for h in range(2):
                row = (r + h) // nf * 8 + (r + h) % nf
                stage[pl.ds(d * SLOTS * 32 + row, SLOTS, stride=32), :] = both[h * SLOTS : (h + 1) * SLOTS]

    @pl.loop(0, slots + 1)
    def _(i):
        table[i] = stage[pl.ds(pl.multiple_of(i * 32, 32), 32), :].astype(BF16)

    acc[...] = jnp.zeros_like(acc)
    src[...] = jnp.zeros_like(src)
    to_smem.wait()

    n = smem[prow, 0]
    for c in loads:
        c.wait()
    sub = lax.broadcasted_iota(I32, (128, 128), 0).astype(F32).astype(BF16)
    yes, no = jnp.ones((128, 128), BF16), jnp.zeros((128, 128), BF16)

    @pl.loop(0, (n + BATCH - 1) // BATCH)
    def _(step):
        where_at, ys = [], []
        for j in range(BATCH):
            v = smem[step // (128 // BATCH), lax.rem(step, 128 // BATCH) * BATCH + j]
            b = v & (blocks - 1)
            slot = v >> shift
            cell = pos_ref[pl.ds(b, 1), :]
            y = cell >> 7
            z = (cell & 127).astype(F32).astype(BF16)
            one = jnp.where(sub == jnp.broadcast_to(z, (128, 128)), yes, no)
            hot[j] = one
            got = jnp.dot(table[slot], one, preferred_element_type=F32)
            upper = jnp.where(y < 1, got[0:8], got[8:16])
            lower = jnp.where(y < 3, got[16:24], got[24:32])
            seen[pl.ds(j * 8, 8), :] = jnp.where(y < 2, upper, lower)
            for f in range(3):
                par[f : f + 1, j, :] = mot_ref[f, pl.ds(b, 1), :]
            par[3:4, j, :] = warm_ref[pl.ds(b, 1), :]
            par[4:5, j, :] = mass_ref[pl.ds(b, 1), :]
            par[5:6, j, :] = mult_ref[pl.ds(b, 1), :]
            where_at.append(slot)
            ys.append(y)
        field = [seen[pl.ds(f, BATCH, stride=8), :] for f in range(5)]
        v0, v1, v2, warm, mass, mult = [par[f] for f in range(6)]
        r0, r1, r2 = field[0] - v0, field[1] - v1, field[2] - v2
        speed_sq = r0 * r0 + r1 * r1 + r2 * r2
        inv_surface = jnp.exp(jnp.log(mass) * (-2.0 / 3.0))
        inverse_tau = 0.8 * (1.0 + 0.15 * jnp.exp(0.3435 * jnp.log(1.0 + speed_sq))) * inv_surface
        relax = 1.0 - jnp.exp(-0.5 * inverse_tau)
        heating = 1.0 / (1.0 + jnp.exp(field[4] - field[3]))
        remain = jnp.exp(-0.3 * heating * inv_surface)
        new_mass = mass * remain
        warming = 1.0 - jnp.exp(-0.25 * inverse_tau)
        new_warm = warm + warming * (field[3] - warm) - 0.5 * (1.0 - remain)
        outs = [mass * v - new_mass * (v + relax * r) for v, r in ((v0, r0), (v1, r1), (v2, r2))]
        outs += [mass * warm - new_mass * new_warm, mass - new_mass]
        for f, o in enumerate(outs):
            src[pl.ds(f, BATCH, stride=8), :] = mult * o
        added = []
        for j in range(BATCH):
            s8 = src[pl.ds(j * 8, 8), :]
            s32 = jnp.concatenate([jnp.where(ys[j] == k, s8, 0.0) for k in range(4)], axis=0).astype(BF16)
            added.append(
                lax.dot_general(s32, hot[j], (((1,), (1,)), ((), ())), preferred_element_type=F32)
            )
        for j in range(BATCH):
            at = pl.ds(pl.multiple_of(where_at[j] * 32, 32), 32)
            acc[at, :] = acc[at, :] + added[j]

    for d in range(nt):
        for r in range(0, rows, 2):
            pair = [
                acc[pl.ds(d * SLOTS * 32 + q // nf * 8 + q % nf, SLOTS, stride=32), :] for q in (r, r + 1)
            ]
            dep_ref[d, r * SLOTS : (r + 2) * SLOTS, :] = jnp.concatenate(pair, axis=0).astype(BF16)


def finish_kernel(
    ng, nt, nf, dep_ref, selt_ref, gas_ref, nu_ref, ylo_ref, yhi_ref, xlo_ref, xhi_ref,
    out_ref, recv, part, tile_s, tile_r, local_sem,
):
    g, t = lax.axis_index("grp"), lax.axis_index("tile")
    peers = [(g, lax.rem(t + k, nt)) for k in range(1, nt)]
    greet(peers)
    copies = []
    for k, peer in enumerate(peers):
        c = pltpu.make_async_remote_copy(
            src_ref=dep_ref.at[peer[1]], dst_ref=recv.at[t], send_sem=tile_s.at[k],
            recv_sem=tile_r.at[k], device_id=peer, device_id_type=MESH,
        )
        c.start()
        copies.append(c)
    slab = pltpu.make_async_copy(dep_ref.at[t], recv.at[t], local_sem)
    slab.start()
    rows, planes, width = gas_ref.shape
    sub = lax.broadcasted_iota(I32, (planes, width), 0)
    lane = lax.broadcasted_iota(I32, (planes, width), 1)
    gas_side = jnp.where(g < ng - 1, 1.0, 0.0).astype(F32)
    has_low = jnp.where(t > 0, 1.0, 0.0).astype(F32)
    has_high = jnp.where(t < nt - 1, 1.0, 0.0).astype(F32)
    x_low = xlo_ref[...].astype(F32) * has_low
    x_high = xhi_ref[...].astype(F32) * has_high
    for r in range(rows):
        mid = gas_ref[r]
        below = gas_ref[r - nf] if r >= nf else ylo_ref[r].astype(F32)
        above = gas_ref[r + nf] if r < rows - nf else yhi_ref[r - (rows - nf)].astype(F32)
        total = below + above
        total += jnp.where(sub == 0, x_low[r : r + 1], pltpu.roll(mid, 1, 0))
        total += jnp.where(sub == planes - 1, x_high[r : r + 1], pltpu.roll(mid, planes - 1, 0))
        total += jnp.where(lane == 0, 0.0, pltpu.roll(mid, 1, 1))
        total += jnp.where(lane == width - 1, 0.0, pltpu.roll(mid, width - 1, 1))
        part[r] = (mid + 0.5 * nu_ref[:, r // nf, :] * (total - 6.0 * mid)) * gas_side
    slab.wait()
    for c in copies:
        c.wait()
    selt = selt_ref[...]
    for r in range(0, rows, 2):
        both = recv[:, r * SLOTS : (r + 2) * SLOTS, :].astype(F32)
        for h in range(2):
            inc = both[:, h * SLOTS : (h + 1) * SLOTS, :].reshape(nt * SLOTS, width).astype(BF16)
            placed = lax.dot_general(
                selt, inc, (((0,), (0,)), ((), ())), preferred_element_type=F32
            )
            q = r + h
            out_ref[q % nf, :, q // nf, :] = part[q] + placed * gas_side


def local(
    flow_fields, turbulent_diffusivity, holder_unit, spray_volume_position, patch_pick_unreduced,
    droplet_motion, droplet_warmth, droplet_weightiness, droplet_multiplicity, living_spray_batches,
):
    ng, nt = lax.axis_size("grp"), lax.axis_size("tile")
    nf, planes, rows_y, width = flow_fields.shape
    rows = nf * rows_y
    slab = jax.ShapeDtypeStruct((nt, rows * SLOTS, width), BF16)
    slab_bytes = nt * rows * SLOTS * width * 2
    dma = pltpu.SemaphoreType.DMA
    edge = jax.ShapeDtypeStruct((rows, width), BF16)
    send, sel, gas, gas_low, first, last, own_row = pl.pallas_call(
        functools.partial(pack_kernel, ng, nt),
        out_shape=(
            slab,
            jax.ShapeDtypeStruct((nt * SLOTS, planes), BF16),
            jax.ShapeDtypeStruct((rows, planes, width), F32),
            jax.ShapeDtypeStruct((rows, planes, width), BF16),
            edge,
            edge,
            jax.ShapeDtypeStruct((1, 1, 128), I32),
        ),
        in_specs=[VMEM] * 2, out_specs=(VMEM,) * 7,
        compiler_params=pltpu.CompilerParams(vmem_limit_bytes=slab_bytes * 2 + (6 << 20)),
        name="pack",
    )(holder_unit.reshape(1, planes), flow_fields)
    halo_y = jax.ShapeDtypeStruct((nf, planes, width), BF16)
    halo_x = jax.ShapeDtypeStruct((rows, width), BF16)
    blocks = spray_volume_position.shape[1]
    slots = nt * SLOTS
    prow = blocks // 128
    bulk = (
        patch_pick_unreduced.reshape(prow, 128), spray_volume_position[0],
        droplet_motion[0].transpose(1, 0, 2), droplet_warmth[0], droplet_weightiness[0],
        droplet_multiplicity[0],
    )
    recv, ylo, yhi, xlo, xhi, own_all = pl.pallas_call(
        functools.partial(exchange_kernel, ng, nt, nf),
        out_shape=(slab, halo_y, halo_y, halo_x, halo_x, jax.ShapeDtypeStruct((nt, ng, 1, 128), I32)),
        in_specs=[VMEM] * 5, out_specs=(VMEM,) * 6,
        scratch_shapes=[
            dma((nt - 1,)), dma((nt - 1,)), dma((ng - 1,)), dma((ng - 1,)),
            dma((nt - 1,)), dma((nt - 1,)), dma((4,)), dma((4,)), dma((2,)),
        ],
        compiler_params=pltpu.CompilerParams(collective_id=0, has_side_effects=True, vmem_limit_bytes=slab_bytes * 2 + (6 << 20)),
        name="exchange",
    )(send, gas_low, first, last, own_row)
    dep = pl.pallas_call(
        functools.partial(parcel_kernel, ng, nt, nf),
        out_shape=slab,
        in_specs=[SMEM] + [VMEM] * 3 + [HBM] * 5, out_specs=VMEM,
        scratch_shapes=[
            pltpu.VMEM((blocks, 128), I32),
            pltpu.VMEM((3, blocks, 128), F32),
            pltpu.VMEM((blocks, 128), F32),
            pltpu.VMEM((blocks, 128), F32),
            pltpu.VMEM((blocks, 128), F32),
            dma((7,)),
            pltpu.VMEM(((slots + 1) * 32, width), F32),
            pltpu.VMEM((slots + 1, 32, width), BF16),
            pltpu.VMEM(((slots + 1) * 32, width), F32),
            pltpu.VMEM((BATCH * 8, width), F32),
            pltpu.VMEM((6, BATCH, width), F32),
            pltpu.VMEM((BATCH * 8, width), F32),
            pltpu.VMEM((BATCH, 128, 128), BF16),
            pltpu.VMEM((prow + 8, 128), I32),
            pltpu.SMEM((prow + 8, 128), I32),
            dma,
        ],
        compiler_params=pltpu.CompilerParams(vmem_limit_bytes=63_900_000),
        name="parcels",
    )(
        living_spray_batches, recv, own_all.reshape(nt * ng, 128), *bulk,
    )
    return pl.pallas_call(
        functools.partial(finish_kernel, ng, nt, nf),
        out_shape=jax.ShapeDtypeStruct((nf, planes, rows_y, width), F32),
        in_specs=[VMEM] * 8, out_specs=VMEM,
        scratch_shapes=[
            pltpu.VMEM((nt, rows * SLOTS, width), BF16), pltpu.VMEM((rows, planes, width), F32),
            dma((nt - 1,)), dma((nt - 1,)), dma,
        ],
        compiler_params=pltpu.CompilerParams(collective_id=1, has_side_effects=True, vmem_limit_bytes=slab_bytes * 2 + (6 << 20)),
        name="finish",
    )(dep, sel, gas, turbulent_diffusivity, ylo, yhi, xlo, xhi)


def solution(mesh):
    in_specs = (
        P(None, "tile", "grp", None),
        P("tile", "grp", None),
        P("grp", "tile", None),
        P("tile", None, None),
        P("tile", None),
        P("tile", None, None, None),
        P("tile", None, None),
        P("tile", None, None),
        P("tile", None, None),
        P("tile"),
    )
    out_specs = P(None, "tile", "grp", None)
    return jax.shard_map(local, mesh=mesh, in_specs=in_specs, out_specs=out_specs, check_vma=False)
```
